128 devices in a mesh: leaf: 128 (over x, y, z, core).
Axes of the slice: x: 4, y: 4, z: 4, core: 2. Of those that a mesh axis runs over, the one named last changes fastest.
Arguments:
- weights: float32 [524288, 128], P('leaf'), may hold values from -6 to 6
- labels: int32 [524288], P('leaf'), may hold values from 0 to 127
- basis: bfloat16 [2048, 64, 256], P('leaf'), may hold values from -0.375 to 0.375
- near_tiles: bfloat16 [2048, 3, 256, 256], P('leaf'), may hold values from -0.21875 to 0.21875
- near_ids: int32 [2048, 2], P('leaf'), may hold values from 0 to 2047, as said below
- transfer: bfloat16 [3968, 64, 64], P('leaf'), may hold values from -0.5 to 0.5
- couplings: bfloat16 [3968, 64, 256], P('leaf'), may hold values from -0.375 to 0.375
- sources: int32 [3968, 4], P('leaf'), may hold values from 0 to 2047, as said below
- coarse_transfer: bfloat16 [124, 64, 64], replicated, may hold values from -0.5 to 0.5
- coarse_couplings: bfloat16 [126, 64, 256], replicated, may hold values from -0.375 to 0.375
- coarse_sources: int32 [126, 4], replicated, may hold values from 0 to 63, as said below
Outputs:
- updated: float32 [524288, 128], P('leaf')
- second_scores: float32 [524288, 128], P('leaf')
The draws below stay inside these ranges and needn't reach their ends.
Inputs may be any that keep to these rules, and one draw needn't show every extreme that they name: `sources`: rows of device q's block name nodes of their row's level, numbered over all devices; the rows of one device name at most 1 nodes held by any single device (counted over all its rows), and some pair of devices reaches 1. `coarse_sources`: entries of a row name a node of that row's coarse level. `near_ids`: each entry lies within 2 leaves of its own leaf and differs from it; distance 2 occurs.
All inputs are finite; a program needn't handle non-finite values.
Results may differ from the reference program's by a relative error of at most 0.025.
Values may be sent and summed in bfloat16 or wider, within the bound.
A program may use at most 128 MiB of HBM per device.

```python
import jax
import jax.numpy as jnp
import numpy as np

LEAF = 256
RANK = 64
CLASSES = 128
CPL = 4
REACH = 2
LEVELS = 5
LEAF_DEV = 16
NODES_DEV = 31
NLEAF = 2048
POINTS = 524288
COARSE = 126
COARSE_MAPS = 124
CAP = 1
N_LEAF = 128


def draw_near_ids(key, part):
    leaves = jnp.arange(NLEAF, dtype=jnp.int32)
    lower = jax.random.randint(jax.random.fold_in(key, 11), (NLEAF,), 1, REACH + 1)
    upper = jax.random.randint(jax.random.fold_in(key, 12), (NLEAF,), 1, REACH + 1)
    lower = jnp.where(leaves % 5 == 2, REACH, lower)
    upper = jnp.where(leaves % 7 == 3, REACH, upper)
    below = jnp.where(leaves - lower >= 0, leaves - lower, leaves + lower)
    above = jnp.where(leaves + upper < NLEAF, leaves + upper, leaves - upper)
    return jnp.stack([below, above], axis=1).astype(jnp.int32)


def draw_sources(key, part):
    row_height = np.concatenate([np.full(LEAF_DEV >> height, height) for height in range(LEVELS)])
    slot_count = jnp.asarray(np.repeat(LEAF_DEV >> row_height, CPL), dtype=jnp.int32)
    slot_total = NODES_DEV * CPL

    def per_device(device):
        subkey = jax.random.fold_in(key, device)
        shuffled = jax.random.permutation(jax.random.fold_in(subkey, 1), N_LEAF * CAP)[:slot_total]
        owner_dev = (shuffled // CAP).astype(jnp.int32)
        raw = jax.random.randint(jax.random.fold_in(subkey, 2), (slot_total,), 0, 1 << 30)
        within = raw % slot_count
        return (owner_dev * slot_count + within).reshape(NODES_DEV, CPL)
    listing = jax.vmap(per_device)(jnp.arange(N_LEAF, dtype=jnp.int32))
    return listing.reshape(N_LEAF * NODES_DEV, CPL).astype(jnp.int32)


def draw_coarse_sources(key, part):
    height_top = int(N_LEAF).bit_length() - 2
    level_sizes = np.concatenate([np.full(N_LEAF >> height, N_LEAF >> height) for height in range(1, height_top + 1)])
    raw = jax.random.randint(key, (N_LEAF - 2, CPL), 0, 1 << 30)
    return (raw % jnp.asarray(level_sizes, dtype=jnp.int32)[:, None]).astype(jnp.int32)


def set_ends(drawn, key, least, largest):
    place = [jax.random.randint(jax.random.fold_in(key, axis), (), 0, length) for axis, length in enumerate(drawn.shape)]
    longest = drawn.shape.index(max(drawn.shape))
    next_to = place[:longest] + [(place[longest] + 1) % drawn.shape[longest]] + place[longest + 1:]
    return drawn.at[tuple(place)].set(least).at[tuple(next_to)].set(largest)


def block_levels(key, shape, shards, least, largest):
    def one(dim, parts):
        heights = jax.random.uniform(jax.random.fold_in(jax.random.fold_in(key, 6), dim), (parts,), jnp.float32, least / len(shards), largest / len(shards))
        return jnp.repeat(jnp.exp(heights), shape[dim] // parts).reshape((-1,) + (1,) * (len(shape) - dim - 1))

    factor_of = one(*shards[0])
    for cut in shards[1:]:
        factor_of = factor_of * one(*cut)
    return factor_of


def bell_draw(own_key, shape, scale, reach, pieces=(), held_as=jnp.bfloat16):
    level = block_levels(own_key, shape, pieces, -0.22, 0.18) if pieces else 1.0
    entries = jax.random.normal(own_key, shape, jnp.float32) * scale * level
    return jnp.minimum(jnp.maximum(entries, -reach), reach).astype(held_as)


def setup_inputs(seed: int = 0) -> dict:
    keys = jax.random.split(jax.random.key(seed), 12)
    weights = bell_draw(keys[0], (POINTS, CLASSES), 1.0, 6.0, ((0, 128),), jnp.float32)
    labels = set_ends(jax.random.randint(keys[1], (POINTS,), 0, CLASSES), jax.random.fold_in(keys[1], 1), 0, CLASSES - 1).astype(jnp.int32)
    basis = bell_draw(keys[2], (NLEAF, RANK, LEAF), LEAF ** -0.5, 0.375, ((0, 128),))
    near_tiles = bell_draw(keys[3], (NLEAF, 3, LEAF, LEAF), (3 * LEAF) ** -0.5, 0.21875, ((0, 128),))
    near_ids = draw_near_ids(jax.random.fold_in(keys[11], 71), 0)
    transfer = bell_draw(keys[5], (N_LEAF * NODES_DEV, RANK, RANK), (2 * RANK) ** -0.5, 0.5, ((0, 128),))
    couplings = bell_draw(keys[6], (N_LEAF * NODES_DEV, RANK, CPL * RANK), (CPL * RANK) ** -0.5, 0.375, ((0, 128),))
    sources = draw_sources(jax.random.fold_in(keys[11], 71), 0)
    coarse_transfer = bell_draw(keys[8], (COARSE_MAPS, RANK, RANK), (2 * RANK) ** -0.5, 0.5)
    coarse_couplings = bell_draw(keys[9], (COARSE, RANK, CPL * RANK), (CPL * RANK) ** -0.5, 0.375)
    coarse_sources = draw_coarse_sources(jax.random.fold_in(keys[11], 71), 0)
    return {"weights": weights, "labels": labels, "basis": basis, "near_tiles": near_tiles, "near_ids": near_ids, "transfer": transfer, "couplings": couplings, "sources": sources, "coarse_transfer": coarse_transfer, "coarse_couplings": coarse_couplings, "coarse_sources": coarse_sources}


step_size = 0.5


def coupling_term(level_coef, mats, lists):
    blocks = level_coef[lists].astype(jnp.float32)
    blocks = blocks.reshape(lists.shape[0], lists.shape[1] * level_coef.shape[1], level_coef.shape[2])
    return jnp.einsum("tab,tbn->tan", mats.astype(jnp.float32), blocks)


def upward(children, mats):
    half = children.shape[0] // 2
    joined = mats.astype(jnp.float32).reshape(half, 2, mats.shape[1], mats.shape[2])
    kids = children.astype(jnp.float32).reshape(half, 2, children.shape[1], children.shape[2])
    return jnp.einsum("jkcp,jkcn->jpn", joined, kids).astype(jnp.bfloat16)


def downward(coupled, mats, parent_field):
    half = parent_field.shape[0]
    joined = mats.astype(jnp.float32).reshape(half, 2, mats.shape[1], mats.shape[2])
    pushed = jnp.einsum("jkcp,jpn->jkcn", joined, parent_field.astype(jnp.float32))
    return (coupled + pushed.reshape(coupled.shape)).astype(jnp.bfloat16)


def operate(point_vals, basis, near_tiles, near_ids, transfer, couplings, sources, coarse_transfer, coarse_couplings, coarse_sources):
    devices = N_LEAF
    node_count = NODES_DEV
    counts = [LEAF_DEV >> height for height in range(LEVELS)]
    starts = [sum(counts[:height]) for height in range(LEVELS)]
    point_rows = point_vals.reshape(NLEAF, LEAF, CLASSES)
    leaf_coef = jnp.einsum("trp,tpn->trn", basis.astype(jnp.float32), point_rows.astype(jnp.float32)).astype(jnp.bfloat16)
    maps_dev = transfer.reshape(devices, node_count, RANK, RANK)
    mats_dev = couplings.reshape(devices, node_count, RANK, CPL * RANK)
    lists_dev = sources.reshape(devices, node_count, CPL)

    def level_rows(array, height):
        part_rows = array[:, starts[height]:starts[height] + counts[height]]
        return part_rows.reshape((devices * counts[height],) + array.shape[2:])

    coefs = [leaf_coef]
    for height in range(LEVELS - 1):
        coefs.append(upward(coefs[-1], level_rows(maps_dev, height)))
    coarse = [coefs[-1]]
    coarse.append(upward(coarse[-1], maps_dev[:, node_count - 1]))
    coarse_levels = devices.bit_length() - 2
    for height in range(1, coarse_levels):
        offset = devices - (devices >> (height - 1))
        level_count = devices >> height
        coarse.append(upward(coarse[-1], coarse_transfer[offset:offset + level_count]))
    node_field = None
    for height in range(coarse_levels, 0, -1):
        offset = devices - (devices >> (height - 1))
        level_count = devices >> height
        coupled = coupling_term(coarse[height], coarse_couplings[offset:offset + level_count], coarse_sources[offset:offset + level_count])
        if height == coarse_levels:
            node_field = coupled.astype(jnp.bfloat16)
        else:
            node_field = downward(coupled, coarse_transfer[offset:offset + level_count], node_field)
    for height in range(LEVELS - 1, -1, -1):
        coupled = coupling_term(coefs[height], level_rows(mats_dev, height), level_rows(lists_dev, height))
        if height == LEVELS - 1:
            mats = maps_dev[:, node_count - 1]
        else:
            mats = level_rows(maps_dev, height)
        node_field = downward(coupled, mats, node_field)
    near_term = jnp.einsum("trp,trn->tpn", basis.astype(jnp.float32), node_field.astype(jnp.float32))
    neighbours = [point_rows, point_rows[near_ids[:, 0]], point_rows[near_ids[:, 1]]]
    for member in range(3):
        near_term = near_term + jnp.einsum("tpq,tqn->tpn", near_tiles[:, member].astype(jnp.float32), neighbours[member].astype(jnp.float32))
    return near_term.reshape(POINTS, CLASSES)


def reference(weights, labels, basis, near_tiles, near_ids, transfer, couplings, sources, coarse_transfer, coarse_couplings, coarse_sources):
    onehot = (labels[:, None] == jnp.arange(CLASSES, dtype=jnp.int32)[None, :]).astype(jnp.float32)
    extra = (basis, near_tiles, near_ids, transfer, couplings, sources, coarse_transfer, coarse_couplings, coarse_sources)
    first_scores = operate(weights.astype(jnp.bfloat16), *extra)
    middle = weights - step_size * (jax.nn.sigmoid(first_scores) - onehot)
    second_scores = operate(middle.astype(jnp.bfloat16), *extra)
    updated = middle - step_size * (jax.nn.sigmoid(second_scores) - onehot)
    return (updated, second_scores)
```

```python
import functools

import jax
import jax.numpy as jnp
from jax import lax
from jax.experimental import pallas as pl
from jax.experimental.pallas import tpu as pltpu
from jax.sharding import PartitionSpec as P

MESH = pl.DeviceIdType.MESH
DEV = 128
LEAVES = 16
LEAF = 256
RANK = 64
NODES = 31
COLS = 128
HALO = 2
COARSE = 126
STARTS = (0, 16, 24, 28, 30)
COARSE_AT = (0, 64, 96, 112, 120, 124)
BATCH = 8
WINDOW = 4
STEP = 37


def mm(a, b):
    return jnp.dot(a, b, preferred_element_type=jnp.float32)


def within(i, count):
    return lax.max(lax.min(i, count - 1), 0)


def coords(me):
    return (
        lax.div(me, 32),
        lax.rem(lax.div(me, 8), 4),
        lax.rem(lax.div(me, 2), 4),
        lax.rem(me, 2),
    )


def partner_at(me, k):
    x, y, z, c = coords(me)
    dx, dy, dz, dc = coords(lax.rem(k * STEP, DEV))
    line = lax.rem(x + dx, 4) * 4 + lax.rem(y + dy, 4)
    return (line * 4 + lax.rem(z + dz, 4)) * 2 + lax.rem(c + dc, 2)


def remote(src, dst, send_sem, recv_sem, device):
    return pltpu.make_async_remote_copy(
        src_ref=src,
        dst_ref=dst,
        send_sem=send_sem,
        recv_sem=recv_sem,
        device_id=(device,),
        device_id_type=MESH,
    )


def take(ref, sem):
    pltpu.make_async_copy(ref, ref, sem).wait()


def kernel(
    sources_s,
    near_ids_s,
    coarse_sources_s,
    sources_v,
    labels_v,
    weights_h,
    basis_h,
    near_h,
    transfer_h,
    couplings_h,
    coarse_transfer_h,
    coarse_couplings_h,
    updated_h,
    scores_h,
    w,
    shift,
    vals0,
    vals1,
    acc,
    near,
    basis,
    basis_t,
    maps,
    maps_t,
    blocks,
    coef,
    field,
    coupled,
    send,
    recv0,
    recv1,
    request,
    requests,
    chosen_v,
    chosen,
    mate_map,
    mate_coef,
    own_coarse,
    coarse0,
    coarse1,
    planes_in,
    planes,
    cmaps,
    cmaps_t,
    cblocks,
    f1_out,
    f1_in,
    in_sem,
    coarse_sem,
    list_sem,
    halo_send,
    halo_recv,
    mate_sem,
    gather_send,
    gather_recv,
    block_send,
    block_recv,
    f1_send,
    f1_recv,
    small_sem,
    out_sem,
):
    me = lax.axis_index("leaf")
    vals, recv, coarse = (vals0, vals1), (recv0, recv1), (coarse0, coarse1)
    x, y, z, c = coords(me)
    line = x * 4 + y
    mate = me + 1 - 2 * c
    is_server = (z == lax.rem(x + y, 4)) & (c == 1 - lax.rem(y, 2))

    barrier = pltpu.get_barrier_semaphore()

    def greet(k, carry):
        pl.semaphore_signal(
            barrier, inc=1, device_id=(partner_at(me, k),), device_id_type=MESH
        )
        return carry

    lax.fori_loop(1, DEV, greet, 0)

    loads = [
        pltpu.make_async_copy(src, dst, in_sem.at[i])
        for i, (src, dst) in enumerate(
            (
                (weights_h, w),
                (basis_h, basis),
                (transfer_h, maps),
                (couplings_h, blocks),
                (near_h, near),
            )
        )
    ]
    for load in loads:
        load.start()

    coarse_rows = (
        (0, 4 * line, 4),
        (4, 64 + 2 * line, 2),
        (6, 96 + line, 1),
        (7, 112 + lax.div(line, 2), 1),
        (8, 120 + lax.div(line, 4), 1),
        (9, 124 + lax.div(line, 8), 1),
    )
    coarse_loads = [
        pltpu.make_async_copy(coarse_transfer_h, planes_in, coarse_sem.at[6])
    ] + [
        pltpu.make_async_copy(
            coarse_couplings_h.at[pl.ds(row, count)],
            cblocks.at[pl.ds(at, count)],
            coarse_sem.at[i],
        )
        for i, (at, row, count) in enumerate(coarse_rows)
    ]

    @pl.when(is_server)
    def _():
        for load in coarse_loads:
            load.start()

    node = lax.broadcasted_iota(jnp.int32, (4, NODES), 1)
    bits = jnp.full((4, NODES), 4, jnp.int32)
    first = jnp.zeros((4, NODES), jnp.int32)
    for height in range(1, 5):
        bits = jnp.where(node >= STARTS[height], 4 - height, bits)
        first = jnp.where(node >= STARTS[height], STARTS[height], first)
    name = sources_v[...]
    owner = lax.shift_right_logical(name, bits)
    row = first + name - lax.shift_left(owner, bits)
    pad = jnp.zeros((4, COLS - NODES), jnp.int32)
    owner = jnp.concatenate([owner, pad], axis=1).astype(jnp.float32)
    row = jnp.concatenate([row, pad], axis=1).astype(jnp.float32)
    device = lax.broadcasted_iota(jnp.int32, (COLS, COLS), 0)
    hits = jnp.zeros((8, COLS), jnp.float32)
    for k in range(4):
        at = jnp.broadcast_to(owner[k : k + 1], (COLS, COLS)).astype(jnp.int32)
        hot = (at == device).astype(jnp.float32).astype(jnp.bfloat16)
        rows = jnp.broadcast_to(row[k : k + 1], (8, COLS)).astype(jnp.bfloat16)
        hits += lax.dot_general(
            rows, hot, (((1,), (1,)), ((), ())), preferred_element_type=jnp.float32
        )
    asked = hits[0:1].astype(jnp.int32)
    request[...] = asked
    requests[pl.ds(me, 1)] = asked.reshape(1, 1, COLS)

    def half_round(t, carry):
        rows = pl.ds(pl.multiple_of(t * LEAF, LEAF), LEAF)
        v = w[rows, :].astype(jnp.bfloat16)
        vals0[t + HALO] = v
        coef[t] = mm(basis[t], v).astype(jnp.bfloat16)
        return carry

    def climb():
        for height in range(4):
            for j in range(LEAVES >> (height + 1)):
                lo = STARTS[height] + 2 * j
                up = STARTS[height + 1] + j
                kids = coef[lo : lo + 2].reshape(2 * RANK, COLS)
                coef[up] = mm(maps_t[up - LEAVES], kids).astype(jnp.bfloat16)

    loads[0].wait()
    loads[1].wait()
    lax.fori_loop(0, LEAVES, half_round, 0, unroll=4)
    loads[2].wait()

    def turn(j, carry):
        lo = 2 * j
        pair = maps[pl.ds(lo, 2)].reshape(2 * RANK, RANK)
        maps_t[j] = pair.astype(jnp.float32).T.astype(jnp.bfloat16)
        return carry

    lax.fori_loop(0, 15, turn, 0)
    climb()

    def turn_basis(t, carry):
        basis_t[t] = basis[t].astype(jnp.float32).T.astype(jnp.bfloat16)
        return carry

    lax.fori_loop(0, LEAVES, turn_basis, 0)

    lane = lax.broadcasted_iota(jnp.int32, (COLS, COLS), 1)

    def mark(i, carry):
        rows = pl.ds(pl.multiple_of(i * COLS, COLS), COLS)
        row = jnp.broadcast_to(labels_v[pl.ds(i, 1), :], (COLS, COLS))
        column = row.astype(jnp.float32).T.astype(jnp.int32)
        shift[rows, :] = jnp.where(column == lane, 0.25, -0.25).astype(jnp.bfloat16)
        return carry

    lax.fori_loop(0, LEAVES * LEAF // COLS, mark, 0)

    loads[3].wait()
    loads[4].wait()
    pl.semaphore_wait(barrier, DEV - 1)

    def halo_copies(phase):
        after = lax.rem(me + 1, DEV)
        before = lax.rem(me + DEV - 1, DEV)
        v = vals[phase]
        return (
            remote(
                v.at[pl.ds(LEAVES, HALO)],
                v.at[pl.ds(0, HALO)],
                halo_send.at[phase, 0],
                halo_recv.at[phase, 0],
                after,
            ),
            remote(
                v.at[pl.ds(HALO, HALO)],
                v.at[pl.ds(LEAVES + HALO, HALO)],
                halo_send.at[phase, 1],
                halo_recv.at[phase, 1],
                before,
            ),
        )

    def server_device(s):
        sx, sy = lax.div(s, 4), lax.rem(s, 4)
        sz = lax.rem(sx + sy, 4)
        return (s * 4 + sz) * 2 + 1 - lax.rem(sy, 2)

    def gather_copy(phase, i):
        return remote(
            own_coarse.at[phase],
            coarse[phase].at[lax.div(me, 2)],
            gather_send.at[phase],
            gather_recv.at[phase],
            server_device(2 * i + c),
        )

    def mate_copy(phase):
        return remote(
            coef.at[NODES - 1],
            mate_coef.at[phase],
            mate_sem.at[phase, 0],
            mate_sem.at[phase, 1],
            mate,
        )

    map_copy = remote(
        maps.at[NODES - 1], mate_map, mate_sem.at[2, 0], mate_sem.at[2, 1], mate
    )

    def list_copy(k):
        return remote(
            request,
            requests.at[me],
            list_sem.at[0],
            list_sem.at[1],
            partner_at(me, k),
        )

    def block_copy(phase, k, batch):
        to = partner_at(me, k)
        return remote(
            send.at[to],
            recv[phase].at[me],
            block_send.at[phase, batch],
            block_recv.at[phase],
            to,
        )

    def send_top(phase):
        mate_copy(phase).wait_recv()
        if phase == 0:
            map_copy.wait_recv()
            pair = jnp.concatenate(
                [
                    jnp.where(c == 0, maps[NODES - 1].astype(jnp.float32), mate_map[...].astype(jnp.float32)),
                    jnp.where(c == 0, mate_map[...].astype(jnp.float32), maps[NODES - 1].astype(jnp.float32)),
                ],
                axis=0,
            )
            maps_t[15] = pair.T.astype(jnp.bfloat16)
        mine = coef[NODES - 1].astype(jnp.float32)
        theirs = mate_coef[phase].astype(jnp.float32)
        kids = jnp.concatenate(
            [jnp.where(c == 0, mine, theirs), jnp.where(c == 0, theirs, mine)], axis=0
        ).astype(jnp.bfloat16)
        own_coarse[phase] = mm(maps_t[15], kids).astype(jnp.bfloat16)
        for i in range(8):
            gather_copy(phase, i).start()

    def fill(lo, hi):
        def one(d, carry):
            send[d] = coef[within(chosen[0, d], NODES)]
            return carry

        lax.fori_loop(lo, hi, one, 0, unroll=8)

    def near_leaf(phase, t):
        base = me * LEAVES - HALO
        a = within(near_ids_s[0, t] - base, LEAVES + 2 * HALO)
        b = within(near_ids_s[1, t] - base, LEAVES + 2 * HALO)
        rows = pl.ds(pl.multiple_of(t * LEAF, LEAF), LEAF)
        total = mm(near[t, 0], vals[phase][t + HALO])
        total += mm(near[t, 1], vals[phase][a])
        total += mm(near[t, 2], vals[phase][b])
        acc[rows, :] = total

    def send_batch(phase, batch):
        def one(i, carry):
            block_copy(phase, batch * BATCH + i, batch).start()
            return carry

        lax.fori_loop(jnp.where(batch == 0, 1, 0), BATCH, one, 0)

    def batch_sent(phase, batch, count=BATCH):
        take(send.at[pl.ds(0, count)], block_send.at[phase, batch])

    def serve(phase):
        table = coarse[phase]
        if phase == 0:
            for load in coarse_loads:
                load.wait()

            def flip(i, carry):
                plane = planes_in[i].astype(jnp.float32).T
                rows = pl.ds(pl.multiple_of(i * (COARSE - 2), 4), COARSE - 2)
                planes[rows, :] = plane
                return carry

            lax.fori_loop(0, RANK, flip, 0, unroll=4)

            def turn_coarse(j, carry):
                for n in (2 * j, 2 * j + 1):
                    one = planes[pl.ds(n, RANK, stride=COARSE - 2), :]
                    cmaps[n] = one.astype(jnp.bfloat16)
                pair = cmaps[pl.ds(2 * j, 2)].reshape(2 * RANK, RANK)
                cmaps_t[j] = pair.astype(jnp.float32).T.astype(jnp.bfloat16)
                return carry

            lax.fori_loop(0, 62, turn_coarse, 0, unroll=2)
        take(table.at[pl.ds(0, 64)], gather_recv.at[phase])
        for level in range(5):
            at, above = COARSE_AT[level], COARSE_AT[level + 1]

            def up(j, carry, at=at, above=above):
                lo = at + 2 * j
                kids = table[pl.ds(lo, 2)].reshape(2 * RANK, COLS)
                turned = cmaps_t[lax.div(lo, 2)]
                table[above + j] = mm(turned, kids).astype(jnp.bfloat16)
                return carry

            count = 32 >> level
            lax.fori_loop(0, count, up, 0, unroll=min(count, 4))

        def term(slot, level, row):
            at = COARSE_AT[level]
            kids = jnp.concatenate(
                [table[at + within(coarse_sources_s[k, row], DEV >> (level + 1))] for k in range(4)], axis=0
            )
            return mm(cblocks[slot], kids)

        rows = [row for _, row, _ in coarse_rows]
        terms = [
            term(slot, level, rows[level] + i)
            for level, (at, _, count) in enumerate(coarse_rows)
            for i, slot in enumerate(range(at, at + count))
        ]
        f = terms[9].astype(jnp.bfloat16)
        for slot, level in ((8, 4), (7, 3), (6, 2)):
            f = (terms[slot] + mm(cmaps[rows[level]], f)).astype(jnp.bfloat16)
        for i in range(2):
            g = (terms[4 + i] + mm(cmaps[rows[1] + i], f)).astype(jnp.bfloat16)
            for j in range(2):
                n = 2 * i + j
                f1_out[phase, n] = (
                    terms[n] + mm(cmaps[rows[0] + n], g)
                ).astype(jnp.bfloat16)
        for o in range(1, 8):
            f1_copy(phase, o).start()
        f1_in[phase] = f1_out[phase, z]

    def f1_copy(phase, o):
        tz = lax.rem(z + o // 2, 4)
        to = (line * 4 + tz) * 2 + lax.rem(c + o % 2, 2)
        return remote(
            f1_out.at[phase, tz],
            f1_in.at[phase],
            f1_send.at[phase],
            f1_recv.at[phase],
            to,
        )

    def exchange(phase):
        for batch in range(WINDOW):
            send_batch(phase, batch)
        for h in halo_copies(phase):
            h.wait_recv()

        def step(t, carry):
            near_leaf(phase, t)
            near_leaf(phase, t + 1)
            for i in range(2):
                batch = t + i + WINDOW

                @pl.when(batch < DEV // BATCH)
                def _():
                    send_batch(phase, batch)

            return carry

        def pair(i, carry):
            return step(2 * i, carry)

        lax.fori_loop(0, 2, pair, 0)

        @pl.when(is_server)
        def _():
            serve(phase)

        lax.fori_loop(2, LEAVES // 2, pair, 0)

    def finish(phase):
        take(recv[phase].at[pl.ds(0, DEV - 1)], block_recv.at[phase])

        def couple(t, bits):
            kids = jnp.concatenate(
                [
                    recv[phase][within(lax.shift_right_logical(sources_s[k, t], bits), DEV)]
                    for k in range(4)
                ],
                axis=0,
            )
            coupled[t] = mm(blocks[t], kids)

        def leaf_pair(t, carry):
            couple(t, 4)
            return carry

        for t in range(NODES - 1, LEAVES - 1, -1):
            height = max(h for h in range(5) if t >= STARTS[h])
            couple(t, 4 - height)
        lax.fori_loop(0, LEAVES, leaf_pair, 0, unroll=4)

        @pl.when(jnp.logical_not(is_server))
        def _():
            take(f1_in.at[phase], f1_recv.at[phase])

        field[NODES - 1] = (
            coupled[NODES - 1] + mm(maps[NODES - 1], f1_in[phase])
        ).astype(jnp.bfloat16)
        for height in range(3, -1, -1):
            for j in range(LEAVES >> (height + 1)):
                lo = STARTS[height] + 2 * j
                pushed = mm(
                    maps[lo : lo + 2].reshape(2 * RANK, RANK),
                    field[STARTS[height + 1] + j],
                )
                both = coupled[lo : lo + 2] + pushed.reshape(2, RANK, COLS)
                field[lo : lo + 2] = both.astype(jnp.bfloat16)

    def first_leaf(t, carry):
        rows = pl.ds(pl.multiple_of(t * LEAF, LEAF), LEAF)
        score = acc[rows, :] + mm(basis_t[t], field[t])
        moved = shift[rows, :].astype(jnp.float32) - 0.25 * jnp.tanh(0.5 * score)
        middle = w[rows, :] + moved
        w[rows, :] = middle
        v = middle.astype(jnp.bfloat16)
        vals1[t + HALO] = v
        coef[t] = mm(basis[t], v).astype(jnp.bfloat16)
        return carry

    def last_leaf(t, carry):
        rows = pl.ds(pl.multiple_of(t * LEAF, LEAF), LEAF)
        score = acc[rows, :] + mm(basis_t[t], field[t])
        acc[rows, :] = score
        moved = shift[rows, :].astype(jnp.float32) - 0.25 * jnp.tanh(0.5 * score)
        w[rows, :] = w[rows, :] + moved
        return carry

    map_copy.start()
    mate_copy(0).start()

    def ask(k, carry):
        list_copy(k).start()
        return carry

    lax.fori_loop(1, DEV, ask, 0)
    for h in halo_copies(0):
        h.start()
    send_top(0)

    take(requests.at[pl.ds(0, DEV - 1)], list_sem.at[1])
    mine = (lax.broadcasted_iota(jnp.int32, (8, DEV), 1) == me).astype(jnp.bfloat16)
    table = requests[...].reshape(DEV, COLS).astype(jnp.float32).astype(jnp.bfloat16)
    wanted = lax.dot_general(
        mine, table, (((1,), (1,)), ((), ())), preferred_element_type=jnp.float32
    )
    chosen_v[...] = jnp.clip(wanted, 0, NODES - 1).astype(jnp.int32)
    small = pltpu.make_async_copy(chosen_v, chosen, small_sem)
    small.start()
    small.wait()

    fill(0, DEV)
    recv0[me] = coef[within(chosen[0, me], NODES)]
    exchange(0)
    finish(0)
    lax.fori_loop(0, LEAVES, first_leaf, 0, unroll=2)

    for batch in range(DEV // BATCH):
        batch_sent(0, batch, BATCH - 1 if batch == 0 else BATCH)
    mate_copy(0).wait_send()
    for h in halo_copies(1):
        h.start()
    climb()
    mate_copy(1).start()
    fill(0, DEV)
    recv1[me] = coef[within(chosen[0, me], NODES)]
    send_top(1)
    exchange(1)
    finish(1)
    lax.fori_loop(0, LEAVES, last_leaf, 0, unroll=2)
    outs = [
        pltpu.make_async_copy(w, updated_h, out_sem.at[0]),
        pltpu.make_async_copy(acc, scores_h, out_sem.at[1]),
    ]
    for out in outs:
        out.start()

    map_copy.wait_send()
    take(requests.at[pl.ds(0, DEV - 1)], list_sem.at[0])
    mate_copy(1).wait_send()
    for batch in range(DEV // BATCH):
        batch_sent(1, batch, BATCH - 1 if batch == 0 else BATCH)
    for phase in range(2):
        for h in halo_copies(phase):
            h.wait_send()
        take(coarse[phase].at[pl.ds(0, 8)], gather_send.at[phase])

        @pl.when(is_server)
        def _():
            take(coarse[phase].at[pl.ds(0, 7)], f1_send.at[phase])

    for out in outs:
        out.wait()


def local(
    weights,
    labels,
    basis,
    near_tiles,
    near_ids,
    transfer,
    couplings,
    sources,
    coarse_transfer,
    coarse_couplings,
    coarse_sources,
):
    bf16, f32, i32 = jnp.bfloat16, jnp.float32, jnp.int32
    points = LEAVES * LEAF
    smem = pl.BlockSpec(memory_space=pltpu.SMEM)
    vmem = pl.BlockSpec(memory_space=pltpu.VMEM)
    hbm = pl.BlockSpec(memory_space=pl.ANY)
    dma = pltpu.SemaphoreType.DMA
    scratch = [
        pltpu.VMEM((points, COLS), f32),
        pltpu.VMEM((points, COLS), bf16),
        pltpu.VMEM((LEAVES + 2 * HALO, LEAF, COLS), bf16),
        pltpu.VMEM((LEAVES + 2 * HALO, LEAF, COLS), bf16),
        pltpu.VMEM((points, COLS), f32),
        pltpu.VMEM((LEAVES, 3, LEAF, LEAF), bf16),
        pltpu.VMEM((LEAVES, RANK, LEAF), bf16),
        pltpu.VMEM((LEAVES, LEAF, RANK), bf16),
        pltpu.VMEM((NODES, RANK, RANK), bf16),
        pltpu.VMEM((16, RANK, 2 * RANK), bf16),
        pltpu.VMEM((NODES, RANK, 4 * RANK), bf16),
        pltpu.VMEM((NODES, RANK, COLS), bf16),
        pltpu.VMEM((NODES, RANK, COLS), bf16),
        pltpu.VMEM((NODES, RANK, COLS), f32),
        pltpu.VMEM((DEV, RANK, COLS), bf16),
        pltpu.VMEM((DEV, RANK, COLS), bf16),
        pltpu.VMEM((DEV, RANK, COLS), bf16),
        pltpu.VMEM((1, COLS), i32),
        pltpu.VMEM((DEV, 1, COLS), i32),
        pltpu.VMEM((8, DEV), i32),
        pltpu.SMEM((8, DEV), i32),
        pltpu.VMEM((RANK, RANK), bf16),
        pltpu.VMEM((2, RANK, COLS), bf16),
        pltpu.VMEM((2, RANK, COLS), bf16),
        pltpu.VMEM((COARSE, RANK, COLS), bf16),
        pltpu.VMEM((COARSE, RANK, COLS), bf16),
        pltpu.VMEM((RANK, RANK, COARSE - 2), bf16),
        pltpu.VMEM(((RANK + 1) * (COARSE - 2), RANK), f32),
        pltpu.VMEM((COARSE - 2, RANK, RANK), bf16),
        pltpu.VMEM((62, RANK, 2 * RANK), bf16),
        pltpu.VMEM((10, RANK, 4 * RANK), bf16),
        pltpu.VMEM((2, 4, RANK, COLS), bf16),
        pltpu.VMEM((2, RANK, COLS), bf16),
        dma((5,)),
        dma((7,)),
        dma((2,)),
        dma((2, 2)),
        dma((2, 2)),
        dma((3, 2)),
        dma((2,)),
        dma((2,)),
        dma((2, DEV // BATCH)),
        dma((2,)),
        dma((2,)),
        dma((2,)),
        dma(()),
        dma((2,)),
    ]
    return pl.pallas_call(
        kernel,
        out_shape=(
            jax.ShapeDtypeStruct((points, COLS), f32),
            jax.ShapeDtypeStruct((points, COLS), f32),
        ),
        in_specs=[smem, smem, smem, vmem, vmem] + [hbm] * 7,
        out_specs=(hbm, hbm),
        scratch_shapes=scratch,
        compiler_params=pltpu.CompilerParams(
            collective_id=0, has_side_effects=True, vmem_limit_bytes=58 << 20
        ),
    )(
        sources.T,
        near_ids.T,
        coarse_sources.T,
        sources.T,
        labels.reshape(points // COLS, COLS),
        weights,
        basis,
        near_tiles,
        transfer,
        couplings,
        coarse_transfer.transpose(1, 2, 0),
        coarse_couplings,
    )


def solution(mesh):
    in_specs = (
        P("leaf", None),
        P("leaf"),
        P("leaf", None, None),
        P("leaf", None, None, None),
        P("leaf", None),
        P("leaf", None, None),
        P("leaf", None, None),
        P("leaf", None),
        P(),
        P(),
        P(),
    )
    out_specs = (P("leaf", None), P("leaf", None))
    return jax.shard_map(local, mesh=mesh, in_specs=in_specs, out_specs=out_specs, check_vma=False)
```

```python
import functools

import jax
import jax.numpy as jnp
from jax import lax
from jax.experimental import pallas as pl
from jax.experimental.pallas import tpu as pltpu
from jax.sharding import PartitionSpec as P

MESH = pl.DeviceIdType.MESH
DEV = 128
LEAVES = 16
LEAF = 256
RANK = 64
NODES = 31
COLS = 128
HALO = 2
COARSE = 126
STARTS = (0, 16, 24, 28, 30)
COARSE_AT = (0, 64, 96, 112, 120, 124)
BATCH = 8
BATCHES = DEV // BATCH


def mm(a, b):
    return jnp.dot(a, b, preferred_element_type=jnp.float32)


def within(i, count):
    return lax.max(lax.min(i, count - 1), 0)


def coords(me):
    return (
        lax.div(me, 32),
        lax.rem(lax.div(me, 8), 4),
        lax.rem(lax.div(me, 2), 4),
        lax.rem(me, 2),
    )


def batch_of(me, b):
    x, y, z, c = coords(me)
    bx, by = lax.div(b, 4), lax.rem(b, 4)
    xs = [lax.rem(x + bx + j, 4) * 32 for j in range(4)]
    ys = [lax.rem(y + by + j, 4) * 8 for j in range(4)]
    zs = [lax.rem(z + j, 4) * 2 for j in range(4)]
    cs = [c, 1 - c]
    return [
        xs[j] + ys[(j + 2 * k) % 4] + zs[j] + cs[k] for j in range(4) for k in range(2)
    ]


def for_all(me, act):
    for device in batch_of(me, 0)[1:]:
        act(device)

    def one(b, carry):
        for device in batch_of(me, b):
            act(device)
        return carry

    lax.fori_loop(1, BATCHES, one, 0)


def remote(src, dst, send_sem, recv_sem, device):
    return pltpu.make_async_remote_copy(
        src_ref=src,
        dst_ref=dst,
        send_sem=send_sem,
        recv_sem=recv_sem,
        device_id=(device,),
        device_id_type=MESH,
    )


def take(ref, sem):
    pltpu.make_async_copy(ref, ref, sem).wait()


def kernel(
    sources_s,
    near_ids_s,
    coarse_sources_s,
    sources_v,
    labels_v,
    weights_h,
    basis_h,
    near_h,
    transfer_h,
    couplings_h,
    coarse_transfer_h,
    coarse_couplings_h,
    updated,
    scores,
    w,
    based,
    shift,
    vals0,
    vals1,
    acc,
    near,
    basis,
    basis_t,
    maps,
    maps_t,
    blocks,
    coef,
    field,
    coupled,
    send,
    recv0,
    recv1,
    request,
    requests,
    chosen_v,
    chosen,
    mate_map,
    mate_coef,
    own_coarse,
    coarse0,
    coarse1,
    planes_in,
    planes,
    cmaps,
    cmaps_t,
    cblocks,
    f1_out,
    f1_in,
    in_sem,
    coarse_sem,
    list_sem,
    halo_send,
    halo_recv,
    mate_sem,
    gather_send,
    gather_recv,
    block_send,
    block_recv,
    f1_send,
    f1_recv,
    small_sem,
):
    me = lax.axis_index("leaf")
    vals, recv, coarse = (vals0, vals1), (recv0, recv1), (coarse0, coarse1)
    x, y, z, c = coords(me)
    line = x * 4 + y
    mate = me + 1 - 2 * c
    is_server = (z == lax.rem(x + y, 4)) & (c == 1 - lax.rem(y, 2))

    barrier = pltpu.get_barrier_semaphore()

    def greet(device):
        pl.semaphore_signal(
            barrier, inc=1, device_id=(device,), device_id_type=MESH
        )

    loads = [
        pltpu.make_async_copy(src, dst, in_sem.at[i])
        for i, (src, dst) in enumerate(
            (
                (weights_h, w),
                (basis_h, basis),
                (transfer_h, maps),
                (couplings_h, blocks),
                (near_h, near),
            )
        )
    ]
    for load in loads:
        load.start()
    for_all(me, greet)

    coarse_rows = (
        (0, 4 * line, 4),
        (4, 64 + 2 * line, 2),
        (6, 96 + line, 1),
        (7, 112 + lax.div(line, 2), 1),
        (8, 120 + lax.div(line, 4), 1),
        (9, 124 + lax.div(line, 8), 1),
    )
    coarse_loads = [
        pltpu.make_async_copy(coarse_transfer_h, planes_in, coarse_sem.at[6])
    ] + [
        pltpu.make_async_copy(
            coarse_couplings_h.at[pl.ds(row, count)],
            cblocks.at[pl.ds(at, count)],
            coarse_sem.at[i],
        )
        for i, (at, row, count) in enumerate(coarse_rows)
    ]

    @pl.when(is_server)
    def _():
        for load in coarse_loads:
            load.start()

    node = lax.broadcasted_iota(jnp.int32, (4, NODES), 1)
    bits = jnp.full((4, NODES), 4, jnp.int32)
    first = jnp.zeros((4, NODES), jnp.int32)
    for height in range(1, 5):
        bits = jnp.where(node >= STARTS[height], 4 - height, bits)
        first = jnp.where(node >= STARTS[height], STARTS[height], first)
    name = sources_v[...]
    owner = lax.shift_right_logical(name, bits)
    row = first + name - lax.shift_left(owner, bits)
    pad = jnp.zeros((4, COLS - NODES), jnp.int32)
    owner = jnp.concatenate([owner, pad], axis=1).astype(jnp.float32)
    row = jnp.concatenate([row, pad], axis=1).astype(jnp.float32)
    device = lax.broadcasted_iota(jnp.int32, (COLS, COLS), 0)
    hits = jnp.zeros((8, COLS), jnp.float32)
    for k in range(4):
        at = jnp.broadcast_to(owner[k : k + 1], (COLS, COLS)).astype(jnp.int32)
        hot = (at == device).astype(jnp.float32).astype(jnp.bfloat16)
        rows = jnp.broadcast_to(row[k : k + 1], (8, COLS)).astype(jnp.bfloat16)
        hits += lax.dot_general(
            rows, hot, (((1,), (1,)), ((), ())), preferred_element_type=jnp.float32
        )
    asked = hits[0:1].astype(jnp.int32)
    request[...] = asked
    requests[pl.ds(me, 1)] = asked.reshape(1, 1, COLS)

    def half_round(t, carry):
        rows = pl.ds(pl.multiple_of(t * LEAF, LEAF), LEAF)
        v = w[rows, :].astype(jnp.bfloat16)
        vals0[t + HALO] = v
        coef[t] = mm(basis[t], v).astype(jnp.bfloat16)
        return carry

    def climb():
        for height in range(4):
            for j in range(LEAVES >> (height + 1)):
                lo = STARTS[height] + 2 * j
                up = STARTS[height + 1] + j
                kids = coef[lo : lo + 2].reshape(2 * RANK, COLS)
                coef[up] = mm(maps_t[up - LEAVES], kids).astype(jnp.bfloat16)

    loads[0].wait()
    loads[1].wait()
    lax.fori_loop(0, LEAVES, half_round, 0, unroll=4)
    loads[2].wait()

    def turn(j, carry):
        lo = 2 * j
        pair = maps[pl.ds(lo, 2)].reshape(2 * RANK, RANK)
        maps_t[j] = pair.astype(jnp.float32).T.astype(jnp.bfloat16)
        return carry

    lax.fori_loop(0, 15, turn, 0, unroll=5)
    climb()

    def turn_basis(t, carry):
        basis_t[t] = basis[t].astype(jnp.float32).T.astype(jnp.bfloat16)
        return carry

    lane = lax.broadcasted_iota(jnp.int32, (COLS, COLS), 1)

    def mark(i, carry):
        rows = pl.ds(pl.multiple_of(i * COLS, COLS), COLS)
        row = jnp.broadcast_to(labels_v[pl.ds(i, 1), :], (COLS, COLS))
        column = row.astype(jnp.float32).T.astype(jnp.int32)
        shift[rows, :] = jnp.where(column == lane, 0.25, -0.25).astype(jnp.bfloat16)
        return carry

    pl.semaphore_wait(barrier, DEV - 1)

    def halo_copies(phase):
        after = lax.rem(me + 1, DEV)
        before = lax.rem(me + DEV - 1, DEV)
        v = vals[phase]
        return (
            remote(
                v.at[pl.ds(LEAVES, HALO)],
                v.at[pl.ds(0, HALO)],
                halo_send.at[phase, 0],
                halo_recv.at[phase, 0],
                after,
            ),
            remote(
                v.at[pl.ds(HALO, HALO)],
                v.at[pl.ds(LEAVES + HALO, HALO)],
                halo_send.at[phase, 1],
                halo_recv.at[phase, 1],
                before,
            ),
        )

    def server_device(s):
        sx, sy = lax.div(s, 4), lax.rem(s, 4)
        sz = lax.rem(sx + sy, 4)
        return (s * 4 + sz) * 2 + 1 - lax.rem(sy, 2)

    def gather_copy(phase, i):
        return remote(
            own_coarse.at[phase],
            coarse[phase].at[lax.div(me, 2)],
            gather_send.at[phase],
            gather_recv.at[phase],
            server_device(2 * i + c),
        )

    def mate_copy(phase):
        return remote(
            coef.at[NODES - 1],
            mate_coef.at[phase],
            mate_sem.at[phase, 0],
            mate_sem.at[phase, 1],
            mate,
        )

    map_copy = remote(
        maps.at[NODES - 1], mate_map, mate_sem.at[2, 0], mate_sem.at[2, 1], mate
    )

    def list_copy(device):
        remote(
            request, requests.at[me], list_sem.at[0], list_sem.at[1], device
        ).start()

    def block_copy(phase, device):
        remote(
            send.at[device],
            recv[phase].at[me],
            block_send.at[phase],
            block_recv.at[phase],
            device,
        ).start()

    def send_top(phase):
        mate_copy(phase).wait_recv()
        if phase == 0:
            map_copy.wait_recv()
            pair = jnp.concatenate(
                [
                    jnp.where(c == 0, maps[NODES - 1].astype(jnp.float32), mate_map[...].astype(jnp.float32)),
                    jnp.where(c == 0, mate_map[...].astype(jnp.float32), maps[NODES - 1].astype(jnp.float32)),
                ],
                axis=0,
            )
            maps_t[15] = pair.T.astype(jnp.bfloat16)
        mine = coef[NODES - 1].astype(jnp.float32)
        theirs = mate_coef[phase].astype(jnp.float32)
        kids = jnp.concatenate(
            [jnp.where(c == 0, mine, theirs), jnp.where(c == 0, theirs, mine)], axis=0
        ).astype(jnp.bfloat16)
        own_coarse[phase] = mm(maps_t[15], kids).astype(jnp.bfloat16)
        for i in range(8):
            gather_copy(phase, i).start()

    def fill(lo, hi):
        def one(d, carry):
            send[d] = coef[within(chosen[0, d], NODES)]
            return carry

        lax.fori_loop(lo, hi, one, 0, unroll=8)

    def near_leaf(phase, t):
        base = me * LEAVES - HALO
        a = within(near_ids_s[0, t] - base, LEAVES + 2 * HALO)
        b = within(near_ids_s[1, t] - base, LEAVES + 2 * HALO)
        rows = pl.ds(pl.multiple_of(t * LEAF, LEAF), LEAF)
        total = mm(near[t, 0], vals[phase][t + HALO])
        total += mm(near[t, 1], vals[phase][a])
        total += mm(near[t, 2], vals[phase][b])
        acc[rows, :] = total

    def send_blocks(phase):
        for_all(me, lambda device: block_copy(phase, device))

    def blocks_sent(phase):
        take(send.at[pl.ds(0, DEV - 1)], block_send.at[phase])

    def prepare_server():
        for load in coarse_loads:
            load.wait()

        def flip(i, carry):
            plane = planes_in[i].astype(jnp.float32).T
            rows = pl.ds(pl.multiple_of(i * (COARSE - 2), 4), COARSE - 2)
            planes[rows, :] = plane
            return carry

        lax.fori_loop(0, RANK, flip, 0, unroll=4)

        def turn_coarse(j, carry):
            for n in (2 * j, 2 * j + 1):
                one = planes[pl.ds(n, RANK, stride=COARSE - 2), :]
                cmaps[n] = one.astype(jnp.bfloat16)
            pair = cmaps[pl.ds(2 * j, 2)].reshape(2 * RANK, RANK)
            cmaps_t[j] = pair.astype(jnp.float32).T.astype(jnp.bfloat16)
            return carry

        lax.fori_loop(0, 62, turn_coarse, 0, unroll=2)

    def serve(phase):
        table = coarse[phase]
        take(table.at[pl.ds(0, 64)], gather_recv.at[phase])
        for level in range(5):
            at, above = COARSE_AT[level], COARSE_AT[level + 1]

            group = min(32 >> level, 8)
            for j in range(0, 32 >> level, group):
                made = [
                    mm(
                        cmaps_t[at // 2 + i],
                        table[at + 2 * i : at + 2 * i + 2].reshape(2 * RANK, COLS),
                    ).astype(jnp.bfloat16)
                    for i in range(j, j + group)
                ]
                for i in range(group):
                    table[above + j + i] = made[i]

        def term(slot, level, row):
            at = COARSE_AT[level]
            kids = jnp.concatenate(
                [table[at + within(coarse_sources_s[k, row], DEV >> (level + 1))] for k in range(4)], axis=0
            )
            return mm(cblocks[slot], kids)

        rows = [row for _, row, _ in coarse_rows]
        terms = [
            term(slot, level, rows[level] + i)
            for level, (at, _, count) in enumerate(coarse_rows)
            for i, slot in enumerate(range(at, at + count))
        ]
        f = terms[9].astype(jnp.bfloat16)
        for slot, level in ((8, 4), (7, 3), (6, 2)):
            f = (terms[slot] + mm(cmaps[rows[level]], f)).astype(jnp.bfloat16)
        for i in range(2):
            g = (terms[4 + i] + mm(cmaps[rows[1] + i], f)).astype(jnp.bfloat16)
            for j in range(2):
                n = 2 * i + j
                f1_out[phase, n] = (
                    terms[n] + mm(cmaps[rows[0] + n], g)
                ).astype(jnp.bfloat16)
        for o in range(1, 8):
            f1_copy(phase, o).start()
        f1_in[phase] = f1_out[phase, z]

    def f1_copy(phase, o):
        tz = lax.rem(z + o // 2, 4)
        to = (line * 4 + tz) * 2 + lax.rem(c + o % 2, 2)
        return remote(
            f1_out.at[phase, tz],
            f1_in.at[phase],
            f1_send.at[phase],
            f1_recv.at[phase],
            to,
        )

    def exchange(phase):
        if phase == 0:
            lax.fori_loop(0, LEAVES, turn_basis, 0, unroll=4)
            lax.fori_loop(0, LEAVES * LEAF // COLS, mark, 0, unroll=4)

        @pl.when(is_server)
        def _():
            serve(phase)

        for h in halo_copies(phase):
            h.wait_recv()
        if phase == 0:
            loads[4].wait()

        def pair(t, carry):
            near_leaf(phase, 2 * t)
            near_leaf(phase, 2 * t + 1)
            return carry

        lax.fori_loop(0, LEAVES // 2, pair, 0)

    def finish(phase):
        if phase == 0:
            loads[3].wait()
        take(recv[phase].at[pl.ds(0, DEV - 1)], block_recv.at[phase])

        def couple(t, bits):
            kids = jnp.concatenate(
                [
                    recv[phase][within(lax.shift_right_logical(sources_s[k, t], bits), DEV)]
                    for k in range(4)
                ],
                axis=0,
            )
            coupled[t] = mm(blocks[t], kids)

        def leaf_pair(t, carry):
            couple(t, 4)
            return carry

        for t in range(NODES - 1, LEAVES - 1, -1):
            height = max(h for h in range(5) if t >= STARTS[h])
            couple(t, 4 - height)
        lax.fori_loop(0, LEAVES, leaf_pair, 0, unroll=4)

        @pl.when(jnp.logical_not(is_server))
        def _():
            take(f1_in.at[phase], f1_recv.at[phase])

        field[NODES - 1] = (
            coupled[NODES - 1] + mm(maps[NODES - 1], f1_in[phase])
        ).astype(jnp.bfloat16)
        for height in range(3, -1, -1):
            for j in range(LEAVES >> (height + 1)):
                lo = STARTS[height] + 2 * j
                pushed = mm(
                    maps[lo : lo + 2].reshape(2 * RANK, RANK),
                    field[STARTS[height + 1] + j],
                )
                both = coupled[lo : lo + 2] + pushed.reshape(2, RANK, COLS)
                field[lo : lo + 2] = both.astype(jnp.bfloat16)

    def first_leaf(t, carry):
        rows = pl.ds(pl.multiple_of(t * LEAF, LEAF), LEAF)
        score = acc[rows, :] + mm(basis_t[t], field[t])
        marked = shift[rows, :].astype(jnp.float32)
        middle = w[rows, :] + (marked - 0.25 * jnp.tanh(0.5 * score))
        based[rows, :] = middle + marked
        v = middle.astype(jnp.bfloat16)
        vals1[t + HALO] = v
        return carry

    def second_coef(t, carry):
        coef[t] = mm(basis[t], vals1[t + HALO]).astype(jnp.bfloat16)
        return carry

    def last_leaf(t, carry):
        rows = pl.ds(pl.multiple_of(t * LEAF, LEAF), LEAF)
        score = acc[rows, :] + mm(basis_t[t], field[t])
        scores[rows, :] = score
        updated[rows, :] = based[rows, :] - 0.25 * jnp.tanh(0.5 * score)
        return carry

    map_copy.start()
    mate_copy(0).start()

    for_all(me, list_copy)

    @pl.when(is_server)
    def _():
        prepare_server()

    take(requests.at[pl.ds(0, DEV - 1)], list_sem.at[1])
    mine = (lax.broadcasted_iota(jnp.int32, (8, DEV), 1) == me).astype(jnp.bfloat16)
    table = requests[...].reshape(DEV, COLS).astype(jnp.float32).astype(jnp.bfloat16)
    wanted = lax.dot_general(
        mine, table, (((1,), (1,)), ((), ())), preferred_element_type=jnp.float32
    )
    chosen_v[...] = jnp.clip(wanted, 0, NODES - 1).astype(jnp.int32)
    small = pltpu.make_async_copy(chosen_v, chosen, small_sem)
    small.start()
    send_top(0)
    for h in halo_copies(0):
        h.start()
    small.wait()
    fill(0, DEV)
    recv0[me] = coef[within(chosen[0, me], NODES)]
    send_blocks(0)
    exchange(0)
    finish(0)
    lax.fori_loop(0, LEAVES, first_leaf, 0, unroll=4)
    for h in halo_copies(1):
        h.start()
    lax.fori_loop(0, LEAVES, second_coef, 0, unroll=4)

    blocks_sent(0)
    mate_copy(0).wait_send()
    climb()
    mate_copy(1).start()
    fill(0, DEV)
    recv1[me] = coef[within(chosen[0, me], NODES)]
    send_top(1)
    send_blocks(1)
    exchange(1)
    finish(1)
    lax.fori_loop(0, LEAVES, last_leaf, 0, unroll=4)

    map_copy.wait_send()
    take(requests.at[pl.ds(0, DEV - 1)], list_sem.at[0])
    mate_copy(1).wait_send()
    blocks_sent(1)
    for phase in range(2):
        for h in halo_copies(phase):
            h.wait_send()
        take(coarse[phase].at[pl.ds(0, 8)], gather_send.at[phase])

        @pl.when(is_server)
        def _():
            take(coarse[phase].at[pl.ds(0, 7)], f1_send.at[phase])


def local(
    weights,
    labels,
    basis,
    near_tiles,
    near_ids,
    transfer,
    couplings,
    sources,
    coarse_transfer,
    coarse_couplings,
    coarse_sources,
):
    bf16, f32, i32 = jnp.bfloat16, jnp.float32, jnp.int32
    points = LEAVES * LEAF
    smem = pl.BlockSpec(memory_space=pltpu.SMEM)
    vmem = pl.BlockSpec(memory_space=pltpu.VMEM)
    hbm = pl.BlockSpec(memory_space=pl.ANY)
    dma = pltpu.SemaphoreType.DMA
    scratch = [
        pltpu.VMEM((points, COLS), f32),
        pltpu.VMEM((points, COLS), f32),
        pltpu.VMEM((points, COLS), bf16),
        pltpu.VMEM((LEAVES + 2 * HALO, LEAF, COLS), bf16),
        pltpu.VMEM((LEAVES + 2 * HALO, LEAF, COLS), bf16),
        pltpu.VMEM((points, COLS), f32),
        pltpu.VMEM((LEAVES, 3, LEAF, LEAF), bf16),
        pltpu.VMEM((LEAVES, RANK, LEAF), bf16),
        pltpu.VMEM((LEAVES, LEAF, RANK), bf16),
        pltpu.VMEM((NODES, RANK, RANK), bf16),
        pltpu.VMEM((16, RANK, 2 * RANK), bf16),
        pltpu.VMEM((NODES, RANK, 4 * RANK), bf16),
        pltpu.VMEM((NODES, RANK, COLS), bf16),
        pltpu.VMEM((NODES, RANK, COLS), bf16),
        pltpu.VMEM((NODES, RANK, COLS), f32),
        pltpu.VMEM((DEV, RANK, COLS), bf16),
        pltpu.VMEM((DEV, RANK, COLS), bf16),
        pltpu.VMEM((DEV, RANK, COLS), bf16),
        pltpu.VMEM((1, COLS), i32),
        pltpu.VMEM((DEV, 1, COLS), i32),
        pltpu.VMEM((8, DEV), i32),
        pltpu.SMEM((8, DEV), i32),
        pltpu.VMEM((RANK, RANK), bf16),
        pltpu.VMEM((2, RANK, COLS), bf16),
        pltpu.VMEM((2, RANK, COLS), bf16),
        pltpu.VMEM((COARSE, RANK, COLS), bf16),
        pltpu.VMEM((COARSE, RANK, COLS), bf16),
        pltpu.VMEM((RANK, RANK, COARSE - 2), bf16),
        pltpu.VMEM(((RANK + 1) * (COARSE - 2), RANK), f32),
        pltpu.VMEM((COARSE - 2, RANK, RANK), bf16),
        pltpu.VMEM((62, RANK, 2 * RANK), bf16),
        pltpu.VMEM((10, RANK, 4 * RANK), bf16),
        pltpu.VMEM((2, 4, RANK, COLS), bf16),
        pltpu.VMEM((2, RANK, COLS), bf16),
        dma((5,)),
        dma((7,)),
        dma((2,)),
        dma((2, 2)),
        dma((2, 2)),
        dma((3, 2)),
        dma((2,)),
        dma((2,)),
        dma((2,)),
        dma((2,)),
        dma((2,)),
        dma((2,)),
        dma(()),
    ]
    return pl.pallas_call(
        kernel,
        out_shape=(
            pltpu.VMEM((points, COLS), f32),
            pltpu.VMEM((points, COLS), f32),
        ),
        in_specs=[smem, smem, smem, vmem, vmem] + [hbm] * 7,
        out_specs=(vmem, vmem),
        scratch_shapes=scratch,
        compiler_params=pltpu.CompilerParams(
            collective_id=0, has_side_effects=True, vmem_limit_bytes=58 << 20
        ),
    )(
        sources.T,
        near_ids.T,
        coarse_sources.T,
        sources.T,
        labels.reshape(points // COLS, COLS),
        weights,
        basis,
        near_tiles,
        transfer,
        couplings,
        coarse_transfer.transpose(1, 2, 0),
        coarse_couplings,
    )


def solution(mesh):
    in_specs = (
        P("leaf", None),
        P("leaf"),
        P("leaf", None, None),
        P("leaf", None, None, None),
        P("leaf", None),
        P("leaf", None, None),
        P("leaf", None, None),
        P("leaf", None),
        P(),
        P(),
        P(),
    )
    out_specs = (P("leaf", None), P("leaf", None))
    return jax.shard_map(local, mesh=mesh, in_specs=in_specs, out_specs=out_specs, check_vma=False)
```

```python
import functools

import jax
import jax.numpy as jnp
from jax import lax
from jax.experimental import pallas as pl
from jax.experimental.pallas import tpu as pltpu
from jax.sharding import PartitionSpec as P

MESH = pl.DeviceIdType.MESH
DEV = 128
LEAVES = 16
LEAF = 256
RANK = 64
NODES = 31
COLS = 128
HALO = 2
COARSE = 126
STARTS = (0, 16, 24, 28, 30)
COARSE_AT = (0, 64, 96, 112, 120, 124)
BATCH = 8
BATCHES = DEV // BATCH


def mm(a, b):
    return jnp.dot(a, b, preferred_element_type=jnp.float32)


def pack(wide, turn):
    group = lax.div(lax.broadcasted_iota(jnp.int32, (16, COLS), 1), 32)
    out = wide[0:16]
    if turn % 4:
        out = pltpu.roll(out, 32 * (turn % 4), 1)
    for g in range(1, 4):
        part = wide[16 * g : 16 * g + 16]
        by = (g + turn) % 4
        if by:
            part = pltpu.roll(part, 32 * by, 1)
        out = jnp.where(group == g, part, out)
    return out.astype(jnp.bfloat16)


def unpack(ref, node):
    part = ref[node].astype(jnp.float32)
    parts = [part] + [pltpu.roll(part, 32 * (4 - g), 1) for g in range(1, 4)]
    return jnp.concatenate(parts, axis=0).astype(jnp.bfloat16)


def join(ref, phase):
    group = lax.div(lax.broadcasted_iota(jnp.int32, (16, COLS), 1), 32)
    parts = [ref[phase, v].astype(jnp.float32) for v in range(4)]
    rows = []
    for g in range(4):
        row = parts[0]
        if g:
            row = pltpu.roll(row, 32 * (4 - g), 1)
        for v in range(1, 4):
            by = (v - g) % 4
            part = pltpu.roll(parts[v], 32 * by, 1) if by else parts[v]
            row = jnp.where(group == v, part, row)
        rows.append(row)
    return jnp.concatenate(rows, axis=0).astype(jnp.bfloat16)


def within(i, count):
    return lax.max(lax.min(i, count - 1), 0)


def coords(me):
    return (
        lax.div(me, 32),
        lax.rem(lax.div(me, 8), 4),
        lax.rem(lax.div(me, 2), 4),
        lax.rem(me, 2),
    )


def batch_of(me, b):
    x, y, z, c = coords(me)
    bx, by = lax.div(b, 4), lax.rem(b, 4)
    xs = [lax.rem(x + bx + j, 4) * 32 for j in range(4)]
    ys = [lax.rem(y + by + j, 4) * 8 for j in range(4)]
    zs = [lax.rem(z + j, 4) * 2 for j in range(4)]
    cs = [c, 1 - c]
    return [
        xs[j] + ys[(j + 2 * k) % 4] + zs[j] + cs[k] for j in range(4) for k in range(2)
    ]


def far_first(me, act):
    x, y, z, c = coords(me)
    xs = [lax.rem(x + j, 4) * 32 for j in range(4)]
    ys = [lax.rem(y + j, 4) * 8 for j in range(4)]
    zs = [lax.rem(z + j, 4) * 2 for j in range(4)]
    cs = [c, 1 - c]
    hops = (0, 1, 2, 1)
    order = sorted(range(1, DEV), key=lambda k: -sum(hops[k >> s & 3] for s in (1, 3, 5)))
    for k in order:
        act(xs[k >> 5] + ys[k >> 3 & 3] + zs[k >> 1 & 3] + cs[k & 1])


def for_all(me, act):
    for device in batch_of(me, 0)[1:]:
        act(device)

    def one(b, carry):
        for device in batch_of(me, b):
            act(device)
        return carry

    lax.fori_loop(1, BATCHES, one, 0)


def remote(src, dst, send_sem, recv_sem, device):
    return pltpu.make_async_remote_copy(
        src_ref=src,
        dst_ref=dst,
        send_sem=send_sem,
        recv_sem=recv_sem,
        device_id=(device,),
        device_id_type=MESH,
    )


def take(ref, sem):
    pltpu.make_async_copy(ref, ref, sem).wait()


def kernel(
    sources_s,
    near_ids_s,
    coarse_sources_s,
    sources_v,
    labels_v,
    weights_h,
    basis_h,
    near_h,
    transfer_h,
    couplings_h,
    coarse_transfer_h,
    coarse_couplings_h,
    updated,
    scores,
    w,
    based,
    shift,
    vals0,
    vals1,
    acc,
    near,
    basis,
    basis_t,
    maps,
    maps_t,
    blocks,
    coef,
    field,
    coupled,
    send,
    recv0,
    recv1,
    request,
    requests,
    chosen_v,
    chosen,
    mate_map,
    mate_coef,
    own_coarse,
    packed0,
    packed1,
    table,
    planes_in,
    planes,
    cmaps,
    cmaps_t,
    cblocks,
    f1_out,
    f1_in,
    in_sem,
    coarse_sem,
    list_sem,
    halo_send,
    halo_recv,
    mate_sem,
    gather_send,
    gather_recv,
    block_send,
    block_recv,
    f1_send,
    f1_recv,
    small_sem,
):
    me = lax.axis_index("leaf")
    vals, recv, packed = (vals0, vals1), (recv0, recv1), (packed0, packed1)
    x, y, z, c = coords(me)
    line = x * 4 + y
    mate = me + 1 - 2 * c
    is_server = c == 1 - lax.rem(y, 2)

    barrier = pltpu.get_barrier_semaphore()

    def greet(device):
        pl.semaphore_signal(
            barrier, inc=1, device_id=(device,), device_id_type=MESH
        )

    loads = [
        pltpu.make_async_copy(src, dst, in_sem.at[i])
        for i, (src, dst) in enumerate(
            (
                (weights_h, w),
                (basis_h, basis),
                (transfer_h, maps),
                (couplings_h, blocks),
                (near_h, near),
            )
        )
    ]
    for load in loads:
        load.start()
    far_first(me, greet)

    coarse_rows = (
        (0, 4 * line, 4),
        (4, 64 + 2 * line, 2),
        (6, 96 + line, 1),
        (7, 112 + lax.div(line, 2), 1),
        (8, 120 + lax.div(line, 4), 1),
        (9, 124 + lax.div(line, 8), 1),
    )
    coarse_loads = [
        pltpu.make_async_copy(coarse_transfer_h, planes_in, coarse_sem.at[6])
    ] + [
        pltpu.make_async_copy(
            coarse_couplings_h.at[pl.ds(row, count)],
            cblocks.at[pl.ds(at, count)],
            coarse_sem.at[i],
        )
        for i, (at, row, count) in enumerate(coarse_rows)
    ]

    @pl.when(is_server)
    def _():
        for load in coarse_loads:
            load.start()

    node = lax.broadcasted_iota(jnp.int32, (4, NODES), 1)
    bits = jnp.full((4, NODES), 4, jnp.int32)
    first = jnp.zeros((4, NODES), jnp.int32)
    for height in range(1, 5):
        bits = jnp.where(node >= STARTS[height], 4 - height, bits)
        first = jnp.where(node >= STARTS[height], STARTS[height], first)
    name = sources_v[...]
    owner = lax.shift_right_logical(name, bits)
    row = first + name - lax.shift_left(owner, bits)
    pad = jnp.zeros((4, COLS - NODES), jnp.int32)
    owner = jnp.concatenate([owner, pad], axis=1).astype(jnp.float32)
    row = jnp.concatenate([row, pad], axis=1).astype(jnp.float32)
    device = lax.broadcasted_iota(jnp.int32, (COLS, COLS), 0)
    hits = jnp.zeros((8, COLS), jnp.float32)
    for k in range(4):
        at = jnp.broadcast_to(owner[k : k + 1], (COLS, COLS)).astype(jnp.int32)
        hot = (at == device).astype(jnp.float32).astype(jnp.bfloat16)
        rows = jnp.broadcast_to(row[k : k + 1], (8, COLS)).astype(jnp.bfloat16)
        hits += lax.dot_general(
            rows, hot, (((1,), (1,)), ((), ())), preferred_element_type=jnp.float32
        )
    asked = hits[0:1].astype(jnp.int32)
    request[...] = asked
    requests[pl.ds(me, 1)] = asked.reshape(1, 1, COLS)

    def half_round(t, carry):
        rows = pl.ds(pl.multiple_of(t * LEAF, LEAF), LEAF)
        v = w[rows, :].astype(jnp.bfloat16)
        vals0[t + HALO] = v
        coef[t] = mm(basis[t], v).astype(jnp.bfloat16)
        return carry

    def climb():
        for height in range(4):
            for j in range(LEAVES >> (height + 1)):
                lo = STARTS[height] + 2 * j
                up = STARTS[height + 1] + j
                kids = coef[lo : lo + 2].reshape(2 * RANK, COLS)
                coef[up] = mm(maps_t[up - LEAVES], kids).astype(jnp.bfloat16)

    loads[0].wait()
    loads[1].wait()
    lax.fori_loop(0, LEAVES, half_round, 0, unroll=4)
    loads[2].wait()

    def turn(j, carry):
        lo = 2 * j
        pair = maps[pl.ds(lo, 2)].reshape(2 * RANK, RANK)
        maps_t[j] = pair.astype(jnp.float32).T.astype(jnp.bfloat16)
        return carry

    lax.fori_loop(0, 15, turn, 0, unroll=5)
    climb()

    def turn_basis(t, carry):
        basis_t[t] = basis[t].astype(jnp.float32).T.astype(jnp.bfloat16)
        return carry

    lane = lax.broadcasted_iota(jnp.int32, (COLS, COLS), 1)

    def mark(i, carry):
        rows = pl.ds(pl.multiple_of(i * COLS, COLS), COLS)
        row = jnp.broadcast_to(labels_v[pl.ds(i, 1), :], (COLS, COLS))
        column = row.astype(jnp.float32).T.astype(jnp.int32)
        shift[rows, :] = jnp.where(column == lane, 0.25, -0.25).astype(jnp.bfloat16)
        return carry

    pl.semaphore_wait(barrier, DEV - 1)

    def halo_copies(phase):
        after = lax.rem(me + 1, DEV)
        before = lax.rem(me + DEV - 1, DEV)
        v = vals[phase]
        return (
            remote(
                v.at[pl.ds(LEAVES, HALO)],
                v.at[pl.ds(0, HALO)],
                halo_send.at[phase, 0],
                halo_recv.at[phase, 0],
                after,
            ),
            remote(
                v.at[pl.ds(HALO, HALO)],
                v.at[pl.ds(LEAVES + HALO, HALO)],
                halo_send.at[phase, 1],
                halo_recv.at[phase, 1],
                before,
            ),
        )

    def gather_copies(phase, i):
        to_line = 2 * i + c
        for v in range(4):
            remote(
                own_coarse.at[phase, v],
                packed[phase].at[lax.div(me, 2)],
                gather_send.at[phase],
                gather_recv.at[phase],
                (to_line * 4 + v) * 2 + 1 - c,
            ).start()

    def mate_copy(phase):
        return remote(
            coef.at[NODES - 1],
            mate_coef.at[phase],
            mate_sem.at[phase, 0],
            mate_sem.at[phase, 1],
            mate,
        )

    map_copy = remote(
        maps.at[NODES - 1], mate_map, mate_sem.at[2, 0], mate_sem.at[2, 1], mate
    )

    def list_copy(device):
        remote(
            request, requests.at[me], list_sem.at[0], list_sem.at[1], device
        ).start()

    def block_copy(phase, device):
        remote(
            send.at[device],
            recv[phase].at[me],
            block_send.at[phase],
            block_recv.at[phase],
            device,
        ).start()

    def send_top(phase):
        mate_copy(phase).wait_recv()
        if phase == 0:
            map_copy.wait_recv()
            pair = jnp.concatenate(
                [
                    jnp.where(c == 0, maps[NODES - 1].astype(jnp.float32), mate_map[...].astype(jnp.float32)),
                    jnp.where(c == 0, mate_map[...].astype(jnp.float32), maps[NODES - 1].astype(jnp.float32)),
                ],
                axis=0,
            )
            maps_t[15] = pair.T.astype(jnp.bfloat16)
        mine = coef[NODES - 1].astype(jnp.float32)
        theirs = mate_coef[phase].astype(jnp.float32)
        kids = jnp.concatenate(
            [jnp.where(c == 0, mine, theirs), jnp.where(c == 0, theirs, mine)], axis=0
        ).astype(jnp.bfloat16)
        made = mm(maps_t[15], kids)
        for v in range(4):
            own_coarse[phase, v] = pack(made, -v)

        def spread(i, carry):
            gather_copies(phase, i)
            return carry

        lax.fori_loop(0, 8, spread, 0)

    def fill(lo, hi):
        def one(d, carry):
            send[d] = coef[within(chosen[0, d], NODES)]
            return carry

        lax.fori_loop(lo, hi, one, 0, unroll=8)

    def near_leaf(phase, t):
        base = me * LEAVES - HALO
        a = within(near_ids_s[0, t] - base, LEAVES + 2 * HALO)
        b = within(near_ids_s[1, t] - base, LEAVES + 2 * HALO)
        rows = pl.ds(pl.multiple_of(t * LEAF, LEAF), LEAF)
        total = mm(near[t, 0], vals[phase][t + HALO])
        total += mm(near[t, 1], vals[phase][a])
        total += mm(near[t, 2], vals[phase][b])
        acc[rows, :] = total

    def send_blocks(phase):
        for_all(me, lambda device: block_copy(phase, device))

    def blocks_sent(phase):
        take(send.at[pl.ds(0, DEV - 1)], block_send.at[phase])

    def prepare_server():
        for load in coarse_loads:
            load.wait()

        def flip(i, carry):
            plane = planes_in[i].astype(jnp.float32).T
            rows = pl.ds(pl.multiple_of(i * (COARSE - 2), 4), COARSE - 2)
            planes[rows, :] = plane
            return carry

        lax.fori_loop(0, RANK, flip, 0, unroll=4)

        def turn_coarse(j, carry):
            for n in (2 * j, 2 * j + 1):
                one = planes[pl.ds(n, RANK, stride=COARSE - 2), :]
                cmaps[n] = one.astype(jnp.bfloat16)
            pair = cmaps[pl.ds(2 * j, 2)].reshape(2 * RANK, RANK)
            cmaps_t[j] = pair.astype(jnp.float32).T.astype(jnp.bfloat16)
            return carry

        lax.fori_loop(0, 62, turn_coarse, 0, unroll=2)

    def serve(phase):
        take(packed[phase], gather_recv.at[phase])

        def open_up(n, carry):
            table[n] = unpack(packed[phase], n)
            return carry

        lax.fori_loop(0, 64, open_up, 0, unroll=8)
        for level in range(5):
            at, above = COARSE_AT[level], COARSE_AT[level + 1]

            group = min(32 >> level, 8)
            for j in range(0, 32 >> level, group):
                made = [
                    mm(
                        cmaps_t[at // 2 + i],
                        table[at + 2 * i : at + 2 * i + 2].reshape(2 * RANK, COLS),
                    ).astype(jnp.bfloat16)
                    for i in range(j, j + group)
                ]
                for i in range(group):
                    table[above + j + i] = made[i]

        def term(slot, level, row):
            at = COARSE_AT[level]
            kids = jnp.concatenate(
                [table[at + within(coarse_sources_s[k, row], DEV >> (level + 1))] for k in range(4)], axis=0
            )
            return mm(cblocks[slot], kids)

        rows = [row for _, row, _ in coarse_rows]
        terms = [
            term(slot, level, rows[level] + i)
            for level, (at, _, count) in enumerate(coarse_rows)
            for i, slot in enumerate(range(at, at + count))
        ]
        f = terms[9].astype(jnp.bfloat16)
        for slot, level in ((8, 4), (7, 3), (6, 2)):
            f = (terms[slot] + mm(cmaps[rows[level]], f)).astype(jnp.bfloat16)
        for i in range(2):
            g = (terms[4 + i] + mm(cmaps[rows[1] + i], f)).astype(jnp.bfloat16)
            for j in range(2):
                n = 2 * i + j
                whole = terms[n] + mm(cmaps[rows[0] + n], g)
                f1_out[phase, n] = pack(whole, 0)
        for o in range(1, 8):
            f1_copy(phase, o).start()
        f1_in[phase, z] = f1_out[phase, z]

    def f1_copy(phase, o):
        tz = lax.rem(z + o // 2, 4)
        to = (line * 4 + tz) * 2 + lax.rem(c + o % 2, 2)
        return remote(
            f1_out.at[phase, tz],
            f1_in.at[phase, z],
            f1_send.at[phase],
            f1_recv.at[phase],
            to,
        )

    def exchange(phase):
        if phase == 0:
            lax.fori_loop(0, LEAVES, turn_basis, 0, unroll=4)
            lax.fori_loop(0, LEAVES * LEAF // COLS, mark, 0, unroll=4)

        if phase == 0:
            loads[4].wait()

            @pl.when(is_server)
            def _():
                serve(phase)

        for h in halo_copies(phase):
            h.wait_recv()

        def pair(t, carry):
            near_leaf(phase, 2 * t)
            near_leaf(phase, 2 * t + 1)
            return carry

        lax.fori_loop(0, LEAVES // 2, pair, 0)
        if phase == 1:

            @pl.when(is_server)
            def _():
                serve(phase)

    def finish(phase):
        if phase == 0:
            loads[3].wait()
        take(recv[phase].at[pl.ds(0, DEV - 1)], block_recv.at[phase])

        def couple(t, bits):
            kids = jnp.concatenate(
                [
                    recv[phase][within(lax.shift_right_logical(sources_s[k, t], bits), DEV)]
                    for k in range(4)
                ],
                axis=0,
            )
            coupled[t] = mm(blocks[t], kids)

        def leaf_pair(t, carry):
            couple(t, 4)
            return carry

        for t in range(NODES - 1, LEAVES - 1, -1):
            height = max(h for h in range(5) if t >= STARTS[h])
            couple(t, 4 - height)
        lax.fori_loop(0, LEAVES, leaf_pair, 0, unroll=4)

        @pl.when(jnp.logical_not(is_server))
        def _():
            take(f1_in.at[phase], f1_recv.at[phase])

        @pl.when(is_server)
        def _():
            take(f1_in.at[phase, pl.ds(0, 3)], f1_recv.at[phase])

        field[NODES - 1] = (
            coupled[NODES - 1] + mm(maps[NODES - 1], join(f1_in, phase))
        ).astype(jnp.bfloat16)
        for height in range(3, -1, -1):
            for j in range(LEAVES >> (height + 1)):
                lo = STARTS[height] + 2 * j
                pushed = mm(
                    maps[lo : lo + 2].reshape(2 * RANK, RANK),
                    field[STARTS[height + 1] + j],
                )
                both = coupled[lo : lo + 2] + pushed.reshape(2, RANK, COLS)
                field[lo : lo + 2] = both.astype(jnp.bfloat16)

    def first_leaf(t, carry):
        rows = pl.ds(pl.multiple_of(t * LEAF, LEAF), LEAF)
        score = acc[rows, :] + mm(basis_t[t], field[t])
        marked = shift[rows, :].astype(jnp.float32)
        middle = w[rows, :] + (marked - 0.25 * jnp.tanh(0.5 * score))
        based[rows, :] = middle + marked
        v = middle.astype(jnp.bfloat16)
        vals1[t + HALO] = v
        return carry

    def second_coef(t, carry):
        coef[t] = mm(basis[t], vals1[t + HALO]).astype(jnp.bfloat16)
        return carry

    def last_leaf(t, carry):
        rows = pl.ds(pl.multiple_of(t * LEAF, LEAF), LEAF)
        score = acc[rows, :] + mm(basis_t[t], field[t])
        scores[rows, :] = score
        updated[rows, :] = based[rows, :] - 0.25 * jnp.tanh(0.5 * score)
        return carry

    map_copy.start()
    mate_copy(0).start()

    far_first(me, list_copy)

    @pl.when(is_server)
    def _():
        prepare_server()

    take(requests.at[pl.ds(0, DEV - 1)], list_sem.at[1])
    mine = (lax.broadcasted_iota(jnp.int32, (8, DEV), 1) == me).astype(jnp.bfloat16)
    asks = requests[...].reshape(DEV, COLS).astype(jnp.float32).astype(jnp.bfloat16)
    wanted = lax.dot_general(
        mine, asks, (((1,), (1,)), ((), ())), preferred_element_type=jnp.float32
    )
    chosen_v[...] = jnp.clip(wanted, 0, NODES - 1).astype(jnp.int32)
    small = pltpu.make_async_copy(chosen_v, chosen, small_sem)
    small.start()
    send_top(0)
    for h in halo_copies(0):
        h.start()
    small.wait()
    fill(0, DEV)
    recv0[me] = coef[within(chosen[0, me], NODES)]
    send_blocks(0)
    exchange(0)
    finish(0)
    lax.fori_loop(0, LEAVES, first_leaf, 0, unroll=4)
    for h in halo_copies(1):
        h.start()
    lax.fori_loop(0, LEAVES, second_coef, 0, unroll=4)

    blocks_sent(0)
    mate_copy(0).wait_send()
    climb()
    mate_copy(1).start()
    fill(0, DEV)
    recv1[me] = coef[within(chosen[0, me], NODES)]
    send_top(1)
    send_blocks(1)
    exchange(1)
    finish(1)
    lax.fori_loop(0, LEAVES, last_leaf, 0, unroll=4)

    map_copy.wait_send()
    take(requests.at[pl.ds(0, DEV - 1)], list_sem.at[0])
    mate_copy(1).wait_send()
    blocks_sent(1)
    for phase in range(2):
        for h in halo_copies(phase):
            h.wait_send()
        take(packed[phase].at[pl.ds(0, 32)], gather_send.at[phase])

        @pl.when(is_server)
        def _():
            take(packed[phase].at[pl.ds(0, 7)], f1_send.at[phase])


def local(
    weights,
    labels,
    basis,
    near_tiles,
    near_ids,
    transfer,
    couplings,
    sources,
    coarse_transfer,
    coarse_couplings,
    coarse_sources,
):
    bf16, f32, i32 = jnp.bfloat16, jnp.float32, jnp.int32
    points = LEAVES * LEAF
    smem = pl.BlockSpec(memory_space=pltpu.SMEM)
    vmem = pl.BlockSpec(memory_space=pltpu.VMEM)
    hbm = pl.BlockSpec(memory_space=pl.ANY)
    dma = pltpu.SemaphoreType.DMA
    scratch = [
        pltpu.VMEM((points, COLS), f32),
        pltpu.VMEM((points, COLS), f32),
        pltpu.VMEM((points, COLS), bf16),
        pltpu.VMEM((LEAVES + 2 * HALO, LEAF, COLS), bf16),
        pltpu.VMEM((LEAVES + 2 * HALO, LEAF, COLS), bf16),
        pltpu.VMEM((points, COLS), f32),
        pltpu.VMEM((LEAVES, 3, LEAF, LEAF), bf16),
        pltpu.VMEM((LEAVES, RANK, LEAF), bf16),
        pltpu.VMEM((LEAVES, LEAF, RANK), bf16),
        pltpu.VMEM((NODES, RANK, RANK), bf16),
        pltpu.VMEM((16, RANK, 2 * RANK), bf16),
        pltpu.VMEM((NODES, RANK, 4 * RANK), bf16),
        pltpu.VMEM((NODES, RANK, COLS), bf16),
        pltpu.VMEM((NODES, RANK, COLS), bf16),
        pltpu.VMEM((NODES, RANK, COLS), f32),
        pltpu.VMEM((DEV, RANK, COLS), bf16),
        pltpu.VMEM((DEV, RANK, COLS), bf16),
        pltpu.VMEM((DEV, RANK, COLS), bf16),
        pltpu.VMEM((1, COLS), i32),
        pltpu.VMEM((DEV, 1, COLS), i32),
        pltpu.VMEM((8, DEV), i32),
        pltpu.SMEM((8, DEV), i32),
        pltpu.VMEM((RANK, RANK), bf16),
        pltpu.VMEM((2, RANK, COLS), bf16),
        pltpu.VMEM((2, 4, 16, COLS), bf16),
        pltpu.VMEM((64, 16, COLS), bf16),
        pltpu.VMEM((64, 16, COLS), bf16),
        pltpu.VMEM((COARSE, RANK, COLS), bf16),
        pltpu.VMEM((RANK, RANK, COARSE - 2), bf16),
        pltpu.VMEM(((RANK + 1) * (COARSE - 2), RANK), f32),
        pltpu.VMEM((COARSE - 2, RANK, RANK), bf16),
        pltpu.VMEM((62, RANK, 2 * RANK), bf16),
        pltpu.VMEM((10, RANK, 4 * RANK), bf16),
        pltpu.VMEM((2, 4, 16, COLS), bf16),
        pltpu.VMEM((2, 4, 16, COLS), bf16),
        dma((5,)),
        dma((7,)),
        dma((2,)),
        dma((2, 2)),
        dma((2, 2)),
        dma((3, 2)),
        dma((2,)),
        dma((2,)),
        dma((2,)),
        dma((2,)),
        dma((2,)),
        dma((2,)),
        dma(()),
    ]
    return pl.pallas_call(
        kernel,
        out_shape=(
            pltpu.VMEM((points, COLS), f32),
            pltpu.VMEM((points, COLS), f32),
        ),
        in_specs=[smem, smem, smem, vmem, vmem] + [hbm] * 7,
        out_specs=(vmem, vmem),
        scratch_shapes=scratch,
        compiler_params=pltpu.CompilerParams(
            collective_id=0, has_side_effects=True, vmem_limit_bytes=58 << 20
        ),
    )(
        sources.T,
        near_ids.T,
        coarse_sources.T,
        sources.T,
        labels.reshape(points // COLS, COLS),
        weights,
        basis,
        near_tiles,
        transfer,
        couplings,
        coarse_transfer.transpose(1, 2, 0),
        coarse_couplings,
    )


def solution(mesh):
    in_specs = (
        P("leaf", None),
        P("leaf"),
        P("leaf", None, None),
        P("leaf", None, None, None),
        P("leaf", None),
        P("leaf", None, None),
        P("leaf", None, None),
        P("leaf", None),
        P(),
        P(),
        P(),
    )
    out_specs = (P("leaf", None), P("leaf", None))
    return jax.shard_map(local, mesh=mesh, in_specs=in_specs, out_specs=out_specs, check_vma=False)
```

```python
import functools

import jax
import jax.numpy as jnp
from jax import lax
from jax.experimental import pallas as pl
from jax.experimental.pallas import tpu as pltpu
from jax.sharding import PartitionSpec as P

MESH = pl.DeviceIdType.MESH
DEV = 128
LEAVES = 16
LEAF = 256
RANK = 64
NODES = 31
COLS = 128
HALO = 2
COARSE = 126
STARTS = (0, 16, 24, 28, 30)
COARSE_AT = (0, 64, 96, 112, 120, 124)
BATCH = 8
BATCHES = DEV // BATCH


def mm(a, b):
    return jnp.dot(a, b, preferred_element_type=jnp.float32)


def pack(wide, turn):
    group = lax.div(lax.broadcasted_iota(jnp.int32, (16, COLS), 1), 32)
    out = wide[0:16]
    if turn % 4:
        out = pltpu.roll(out, 32 * (turn % 4), 1)
    for g in range(1, 4):
        part = wide[16 * g : 16 * g + 16]
        by = (g + turn) % 4
        if by:
            part = pltpu.roll(part, 32 * by, 1)
        out = jnp.where(group == g, part, out)
    return out.astype(jnp.bfloat16)


def unpack(ref, node):
    part = ref[node].astype(jnp.float32)
    parts = [part] + [pltpu.roll(part, 32 * (4 - g), 1) for g in range(1, 4)]
    return jnp.concatenate(parts, axis=0).astype(jnp.bfloat16)


def join(ref, phase):
    group = lax.div(lax.broadcasted_iota(jnp.int32, (16, COLS), 1), 32)
    parts = [ref[phase, v].astype(jnp.float32) for v in range(4)]
    rows = []
    for g in range(4):
        row = parts[0]
        if g:
            row = pltpu.roll(row, 32 * (4 - g), 1)
        for v in range(1, 4):
            by = (v - g) % 4
            part = pltpu.roll(parts[v], 32 * by, 1) if by else parts[v]
            row = jnp.where(group == v, part, row)
        rows.append(row)
    return jnp.concatenate(rows, axis=0).astype(jnp.bfloat16)


def within(i, count):
    return lax.max(lax.min(i, count - 1), 0)


def coords(me):
    return (
        lax.div(me, 32),
        lax.rem(lax.div(me, 8), 4),
        lax.rem(lax.div(me, 2), 4),
        lax.rem(me, 2),
    )


def batch_of(me, b):
    x, y, z, c = coords(me)
    bx, by = lax.div(b, 4), lax.rem(b, 4)
    xs = [lax.rem(x + bx + j, 4) * 32 for j in range(4)]
    ys = [lax.rem(y + by + j, 4) * 8 for j in range(4)]
    zs = [lax.rem(z + j, 4) * 2 for j in range(4)]
    cs = [c, 1 - c]
    return [
        xs[j] + ys[(j + 2 * k) % 4] + zs[j] + cs[k] for j in range(4) for k in range(2)
    ]


def far_first(me, act):
    x, y, z, c = coords(me)
    xs = [lax.rem(x + j, 4) * 32 for j in range(4)]
    ys = [lax.rem(y + j, 4) * 8 for j in range(4)]
    zs = [lax.rem(z + j, 4) * 2 for j in range(4)]
    cs = [c, 1 - c]
    hops = (0, 1, 2, 1)
    order = sorted(range(1, DEV), key=lambda k: -sum(hops[k >> s & 3] for s in (1, 3, 5)))
    for k in order:
        act(xs[k >> 5] + ys[k >> 3 & 3] + zs[k >> 1 & 3] + cs[k & 1])


def for_some(me, act, lo, hi):
    if lo == 0:
        for device in batch_of(me, 0)[1:]:
            act(device)
        lo = 1

    def one(b, carry):
        for device in batch_of(me, b):
            act(device)
        return carry

    lax.fori_loop(lo, hi, one, 0)


def remote(src, dst, send_sem, recv_sem, device):
    return pltpu.make_async_remote_copy(
        src_ref=src,
        dst_ref=dst,
        send_sem=send_sem,
        recv_sem=recv_sem,
        device_id=(device,),
        device_id_type=MESH,
    )


def take(ref, sem):
    pltpu.make_async_copy(ref, ref, sem).wait()


def kernel(
    sources_h,
    near_ids_h,
    coarse_sources_h,
    labels_h,
    weights_h,
    basis_h,
    near_h,
    transfer_h,
    couplings_h,
    coarse_transfer_h,
    coarse_couplings_h,
    based,
    acc,
    field,
    basis_t,
    sources_s,
    near_ids_s,
    coarse_sources_s,
    sources_v,
    labels_v,
    w,
    shift,
    vals0,
    vals1,
    near,
    basis,
    maps,
    maps_t,
    blocks,
    coef,
    coupled,
    send,
    recv0,
    recv1,
    request,
    requests,
    chosen_v,
    chosen,
    mate_map,
    mate_coef,
    own_coarse,
    packed0,
    packed1,
    table,
    planes_in,
    planes,
    cmaps,
    cmaps_t,
    cblocks,
    f1_out,
    f1_in,
    in_sem,
    coarse_sem,
    list_sem,
    halo_send,
    halo_recv,
    mate_sem,
    gather_send,
    gather_recv,
    block_send,
    block_recv,
    f1_send,
    f1_recv,
    small_sem,
):
    me = lax.axis_index("leaf")
    vals, recv, packed = (vals0, vals1), (recv0, recv1), (packed0, packed1)
    x, y, z, c = coords(me)
    line = x * 4 + y
    mate = me + 1 - 2 * c
    is_server = c == 1 - lax.rem(y, 2)

    barrier = pltpu.get_barrier_semaphore()

    def greet(device):
        pl.semaphore_signal(
            barrier, inc=1, device_id=(device,), device_id_type=MESH
        )

    loads = [
        pltpu.make_async_copy(src, dst, in_sem.at[i])
        for i, (src, dst) in enumerate(
            (
                (sources_h, sources_v),
                (weights_h, w),
                (basis_h, basis),
                (transfer_h, maps),
                (couplings_h, blocks),
                (sources_h, sources_s),
                (near_ids_h, near_ids_s),
                (coarse_sources_h, coarse_sources_s),
                (labels_h, labels_v),
                (near_h, near),
            )
        )
    ]
    for load in loads:
        load.start()
    far_first(me, greet)

    coarse_rows = (
        (0, 4 * line, 4),
        (4, 64 + 2 * line, 2),
        (6, 96 + line, 1),
        (7, 112 + lax.div(line, 2), 1),
        (8, 120 + lax.div(line, 4), 1),
        (9, 124 + lax.div(line, 8), 1),
    )
    coarse_loads = [
        pltpu.make_async_copy(coarse_transfer_h, planes_in, coarse_sem.at[6])
    ] + [
        pltpu.make_async_copy(
            coarse_couplings_h.at[pl.ds(row, count)],
            cblocks.at[pl.ds(at, count)],
            coarse_sem.at[i],
        )
        for i, (at, row, count) in enumerate(coarse_rows)
    ]

    @pl.when(is_server)
    def _():
        for load in coarse_loads:
            load.start()

    node = lax.broadcasted_iota(jnp.int32, (4, NODES), 1)
    bits = jnp.full((4, NODES), 4, jnp.int32)
    first = jnp.zeros((4, NODES), jnp.int32)
    for height in range(1, 5):
        bits = jnp.where(node >= STARTS[height], 4 - height, bits)
        first = jnp.where(node >= STARTS[height], STARTS[height], first)
    loads[0].wait()
    name = sources_v[...]
    owner = lax.shift_right_logical(name, bits)
    row = first + name - lax.shift_left(owner, bits)
    pad = jnp.zeros((4, COLS - NODES), jnp.int32)
    owner = jnp.concatenate([owner, pad], axis=1).astype(jnp.float32)
    row = jnp.concatenate([row, pad], axis=1).astype(jnp.float32)
    device = lax.broadcasted_iota(jnp.int32, (COLS, COLS), 0)
    hits = jnp.zeros((8, COLS), jnp.float32)
    for k in range(4):
        at = jnp.broadcast_to(owner[k : k + 1], (COLS, COLS)).astype(jnp.int32)
        hot = (at == device).astype(jnp.float32).astype(jnp.bfloat16)
        rows = jnp.broadcast_to(row[k : k + 1], (8, COLS)).astype(jnp.bfloat16)
        hits += lax.dot_general(
            rows, hot, (((1,), (1,)), ((), ())), preferred_element_type=jnp.float32
        )
    asked = hits[0:1].astype(jnp.int32)
    request[...] = asked
    requests[pl.ds(me, 1)] = asked.reshape(1, 1, COLS)

    def half_round(t, carry):
        rows = pl.ds(pl.multiple_of(t * LEAF, LEAF), LEAF)
        v = w[rows, :].astype(jnp.bfloat16)
        vals0[t + HALO] = v
        coef[t] = mm(basis[t], v).astype(jnp.bfloat16)
        return carry

    def climb():
        for height in range(4):
            for j in range(LEAVES >> (height + 1)):
                lo = STARTS[height] + 2 * j
                up = STARTS[height + 1] + j
                kids = coef[lo : lo + 2].reshape(2 * RANK, COLS)
                coef[up] = mm(maps_t[up - LEAVES], kids).astype(jnp.bfloat16)

    loads[1].wait()
    loads[2].wait()
    lax.fori_loop(0, LEAVES, half_round, 0, unroll=4)
    loads[3].wait()

    def turn(j, carry):
        lo = 2 * j
        pair = maps[pl.ds(lo, 2)].reshape(2 * RANK, RANK)
        maps_t[j] = pair.astype(jnp.float32).T.astype(jnp.bfloat16)
        return carry

    lax.fori_loop(0, 15, turn, 0, unroll=5)
    climb()

    def turn_basis(t, carry):
        basis_t[t] = basis[t].astype(jnp.float32).T.astype(jnp.bfloat16)
        return carry

    lane = lax.broadcasted_iota(jnp.int32, (COLS, COLS), 1)

    def mark(i, carry):
        rows = pl.ds(pl.multiple_of(i * COLS, COLS), COLS)
        row = jnp.broadcast_to(labels_v[pl.ds(i, 1), :], (COLS, COLS))
        column = row.astype(jnp.float32).T.astype(jnp.int32)
        shift[rows, :] = jnp.where(column == lane, 0.25, -0.25).astype(jnp.bfloat16)
        return carry

    for load in loads[4:9]:
        load.wait()
    pl.semaphore_wait(barrier, DEV - 1)

    def halo_copies(phase):
        after = lax.rem(me + 1, DEV)
        before = lax.rem(me + DEV - 1, DEV)
        v = vals[phase]
        return (
            remote(
                v.at[pl.ds(LEAVES, HALO)],
                v.at[pl.ds(0, HALO)],
                halo_send.at[phase, 0],
                halo_recv.at[phase, 0],
                after,
            ),
            remote(
                v.at[pl.ds(HALO, HALO)],
                v.at[pl.ds(LEAVES + HALO, HALO)],
                halo_send.at[phase, 1],
                halo_recv.at[phase, 1],
                before,
            ),
        )

    def gather_copies(phase, i):
        to_line = 2 * i + c
        for v in range(4):
            remote(
                own_coarse.at[phase, v],
                packed[phase].at[lax.div(me, 2)],
                gather_send.at[phase],
                gather_recv.at[phase],
                (to_line * 4 + v) * 2 + 1 - c,
            ).start()

    def mate_copy(phase):
        return remote(
            coef.at[NODES - 1],
            mate_coef.at[phase],
            mate_sem.at[phase, 0],
            mate_sem.at[phase, 1],
            mate,
        )

    map_copy = remote(
        maps.at[NODES - 1], mate_map, mate_sem.at[2, 0], mate_sem.at[2, 1], mate
    )

    def list_copy(device):
        remote(
            request, requests.at[me], list_sem.at[0], list_sem.at[1], device
        ).start()

    def block_copy(phase, device):
        remote(
            send.at[device],
            recv[phase].at[me],
            block_send.at[phase],
            block_recv.at[phase],
            device,
        ).start()

    def send_top(phase):
        mate_copy(phase).wait_recv()
        if phase == 0:
            map_copy.wait_recv()
            pair = jnp.concatenate(
                [
                    jnp.where(c == 0, maps[NODES - 1].astype(jnp.float32), mate_map[...].astype(jnp.float32)),
                    jnp.where(c == 0, mate_map[...].astype(jnp.float32), maps[NODES - 1].astype(jnp.float32)),
                ],
                axis=0,
            )
            maps_t[15] = pair.T.astype(jnp.bfloat16)
        mine = coef[NODES - 1].astype(jnp.float32)
        theirs = mate_coef[phase].astype(jnp.float32)
        kids = jnp.concatenate(
            [jnp.where(c == 0, mine, theirs), jnp.where(c == 0, theirs, mine)], axis=0
        ).astype(jnp.bfloat16)
        made = mm(maps_t[15], kids)
        for v in range(4):
            own_coarse[phase, v] = pack(made, -v)

        def spread(i, carry):
            gather_copies(phase, i)
            return carry

        lax.fori_loop(0, 8, spread, 0)

    def fill(lo, hi):
        def one(d, carry):
            send[d] = coef[within(chosen[0, d], NODES)]
            return carry

        lax.fori_loop(lo, hi, one, 0, unroll=8)

    def near_leaf(phase, t):
        base = me * LEAVES - HALO
        a = within(near_ids_s[0, t] - base, LEAVES + 2 * HALO)
        b = within(near_ids_s[1, t] - base, LEAVES + 2 * HALO)
        rows = pl.ds(pl.multiple_of(t * LEAF, LEAF), LEAF)
        total = mm(near[t, 0], vals[phase][t + HALO])
        total += mm(near[t, 1], vals[phase][a])
        total += mm(near[t, 2], vals[phase][b])
        acc[rows, :] = total

    def send_blocks(phase, lo, hi):
        for_some(me, lambda device: block_copy(phase, device), lo, hi)

    def blocks_sent(phase):
        take(send.at[pl.ds(0, DEV - 1)], block_send.at[phase])

    def prepare_server():
        for load in coarse_loads:
            load.wait()

        def flip(i, carry):
            plane = planes_in[i].astype(jnp.float32).T
            rows = pl.ds(pl.multiple_of(i * (COARSE - 2), 4), COARSE - 2)
            planes[rows, :] = plane
            return carry

        lax.fori_loop(0, RANK, flip, 0, unroll=4)

        def turn_coarse(j, carry):
            for n in (2 * j, 2 * j + 1):
                one = planes[pl.ds(n, RANK, stride=COARSE - 2), :]
                cmaps[n] = one.astype(jnp.bfloat16)
            pair = cmaps[pl.ds(2 * j, 2)].reshape(2 * RANK, RANK)
            cmaps_t[j] = pair.astype(jnp.float32).T.astype(jnp.bfloat16)
            return carry

        lax.fori_loop(0, 62, turn_coarse, 0, unroll=2)

    def serve(phase):
        take(packed[phase], gather_recv.at[phase])

        def open_up(n, carry):
            table[n] = unpack(packed[phase], n)
            return carry

        lax.fori_loop(0, 64, open_up, 0, unroll=8)
        for level in range(5):
            at, above = COARSE_AT[level], COARSE_AT[level + 1]

            group = min(32 >> level, 8)
            for j in range(0, 32 >> level, group):
                made = [
                    mm(
                        cmaps_t[at // 2 + i],
                        table[at + 2 * i : at + 2 * i + 2].reshape(2 * RANK, COLS),
                    ).astype(jnp.bfloat16)
                    for i in range(j, j + group)
                ]
                for i in range(group):
                    table[above + j + i] = made[i]

        def term(slot, level, row):
            at = COARSE_AT[level]
            kids = jnp.concatenate(
                [table[at + within(coarse_sources_s[k, row], DEV >> (level + 1))] for k in range(4)], axis=0
            )
            return mm(cblocks[slot], kids)

        rows = [row for _, row, _ in coarse_rows]
        terms = [
            term(slot, level, rows[level] + i)
            for level, (at, _, count) in enumerate(coarse_rows)
            for i, slot in enumerate(range(at, at + count))
        ]
        f = terms[9].astype(jnp.bfloat16)
        for slot, level in ((8, 4), (7, 3), (6, 2)):
            f = (terms[slot] + mm(cmaps[rows[level]], f)).astype(jnp.bfloat16)
        for i in range(2):
            g = (terms[4 + i] + mm(cmaps[rows[1] + i], f)).astype(jnp.bfloat16)
            for j in range(2):
                n = 2 * i + j
                whole = terms[n] + mm(cmaps[rows[0] + n], g)
                f1_out[phase, n] = pack(whole, 0)
        for o in range(1, 8):
            f1_copy(phase, o).start()
        f1_in[phase, z] = f1_out[phase, z]

    def f1_copy(phase, o):
        tz = lax.rem(z + o // 2, 4)
        to = (line * 4 + tz) * 2 + lax.rem(c + o % 2, 2)
        return remote(
            f1_out.at[phase, tz],
            f1_in.at[phase, z],
            f1_send.at[phase],
            f1_recv.at[phase],
            to,
        )

    def exchange(phase):
        if phase == 0:
            lax.fori_loop(0, LEAVES, turn_basis, 0, unroll=4)
            lax.fori_loop(0, LEAVES * LEAF // COLS, mark, 0, unroll=4)

        if phase == 0:
            loads[9].wait()

            @pl.when(is_server)
            def _():
                serve(phase)

        for h in halo_copies(phase):
            h.wait_recv()

        def pair(t, carry):
            near_leaf(phase, 2 * t)
            near_leaf(phase, 2 * t + 1)
            return carry

        lax.fori_loop(0, LEAVES // 2, pair, 0)
        if phase == 1:

            @pl.when(is_server)
            def _():
                serve(phase)

    def finish(phase):
        take(recv[phase].at[pl.ds(0, DEV - 1)], block_recv.at[phase])

        def couple(t, bits):
            kids = jnp.concatenate(
                [
                    recv[phase][within(lax.shift_right_logical(sources_s[k, t], bits), DEV)]
                    for k in range(4)
                ],
                axis=0,
            )
            coupled[t] = mm(blocks[t], kids)

        def leaf_pair(t, carry):
            couple(t, 4)
            return carry

        for t in range(NODES - 1, LEAVES - 1, -1):
            height = max(h for h in range(5) if t >= STARTS[h])
            couple(t, 4 - height)
        lax.fori_loop(0, LEAVES, leaf_pair, 0, unroll=4)

        @pl.when(jnp.logical_not(is_server))
        def _():
            take(f1_in.at[phase], f1_recv.at[phase])

        @pl.when(is_server)
        def _():
            take(f1_in.at[phase, pl.ds(0, 3)], f1_recv.at[phase])

        field[NODES - 1] = (
            coupled[NODES - 1] + mm(maps[NODES - 1], join(f1_in, phase))
        ).astype(jnp.bfloat16)
        for height in range(3, -1, -1):
            for j in range(LEAVES >> (height + 1)):
                lo = STARTS[height] + 2 * j
                pushed = mm(
                    maps[lo : lo + 2].reshape(2 * RANK, RANK),
                    field[STARTS[height + 1] + j],
                )
                both = coupled[lo : lo + 2] + pushed.reshape(2, RANK, COLS)
                field[lo : lo + 2] = both.astype(jnp.bfloat16)

    def first_leaf(t, carry):
        rows = pl.ds(pl.multiple_of(t * LEAF, LEAF), LEAF)
        score = acc[rows, :] + mm(basis_t[t], field[t])
        marked = shift[rows, :].astype(jnp.float32)
        middle = w[rows, :] + (marked - 0.25 * jnp.tanh(0.5 * score))
        based[rows, :] = middle + marked
        v = middle.astype(jnp.bfloat16)
        vals1[t + HALO] = v
        return carry

    def second_coef(t, carry):
        coef[t] = mm(basis[t], vals1[t + HALO]).astype(jnp.bfloat16)
        return carry

    map_copy.start()
    mate_copy(0).start()

    far_first(me, list_copy)

    @pl.when(is_server)
    def _():
        prepare_server()

    take(requests.at[pl.ds(0, DEV - 1)], list_sem.at[1])
    mine = (lax.broadcasted_iota(jnp.int32, (8, DEV), 1) == me).astype(jnp.bfloat16)
    asks = requests[...].reshape(DEV, COLS).astype(jnp.float32).astype(jnp.bfloat16)
    wanted = lax.dot_general(
        mine, asks, (((1,), (1,)), ((), ())), preferred_element_type=jnp.float32
    )
    chosen_v[...] = jnp.clip(wanted, 0, NODES - 1).astype(jnp.int32)
    small = pltpu.make_async_copy(chosen_v, chosen, small_sem)
    small.start()
    send_top(0)
    for h in halo_copies(0):
        h.start()
    small.wait()
    fill(0, DEV)
    recv0[me] = coef[within(chosen[0, me], NODES)]
    send_blocks(0, 0, BATCHES)
    exchange(0)
    finish(0)
    lax.fori_loop(0, LEAVES, first_leaf, 0, unroll=4)
    for h in halo_copies(1):
        h.start()
    lax.fori_loop(0, LEAVES, second_coef, 0, unroll=4)

    blocks_sent(0)
    mate_copy(0).wait_send()
    climb()
    mate_copy(1).start()
    fill(0, DEV)
    recv1[me] = coef[within(chosen[0, me], NODES)]
    send_blocks(1, 0, 2)
    send_top(1)
    send_blocks(1, 2, BATCHES)
    exchange(1)
    finish(1)

    map_copy.wait_send()
    take(requests.at[pl.ds(0, DEV - 1)], list_sem.at[0])
    mate_copy(1).wait_send()
    blocks_sent(1)
    for phase in range(2):
        for h in halo_copies(phase):
            h.wait_send()
        take(packed[phase].at[pl.ds(0, 32)], gather_send.at[phase])

        @pl.when(is_server)
        def _():
            take(packed[phase].at[pl.ds(0, 7)], f1_send.at[phase])


def last_kernel(based, near_term, field, basis_t, updated_h, scores_h, updated, scores, sem):
    copies = []
    for part in range(4):
        for t in range(4 * part, 4 * part + 4):
            rows = pl.ds(t * LEAF, LEAF)
            score = near_term[rows, :] + mm(basis_t[t], field[t])
            scores[rows, :] = score
            updated[rows, :] = based[rows, :] - 0.25 * jnp.tanh(0.5 * score)
        rows = pl.ds(4 * part * LEAF, 4 * LEAF)
        for i, (src, dst) in enumerate(((updated, updated_h), (scores, scores_h))):
            copies.append(
                pltpu.make_async_copy(src.at[rows], dst.at[rows], sem.at[i, part])
            )
            copies[-1].start()
    for copy in copies:
        copy.wait()


def local(
    weights,
    labels,
    basis,
    near_tiles,
    near_ids,
    transfer,
    couplings,
    sources,
    coarse_transfer,
    coarse_couplings,
    coarse_sources,
):
    bf16, f32, i32 = jnp.bfloat16, jnp.float32, jnp.int32
    points = LEAVES * LEAF
    vmem = pl.BlockSpec(memory_space=pltpu.VMEM)
    hbm = pl.BlockSpec(memory_space=pl.ANY)
    dma = pltpu.SemaphoreType.DMA
    scratch = [
        pltpu.SMEM((4, NODES), i32),
        pltpu.SMEM((2, LEAVES), i32),
        pltpu.SMEM((4, COARSE), i32),
        pltpu.VMEM((4, NODES), i32),
        pltpu.VMEM((points // COLS, COLS), i32),
        pltpu.VMEM((points, COLS), f32),
        pltpu.VMEM((points, COLS), bf16),
        pltpu.VMEM((LEAVES + 2 * HALO, LEAF, COLS), bf16),
        pltpu.VMEM((LEAVES + 2 * HALO, LEAF, COLS), bf16),
        pltpu.VMEM((LEAVES, 3, LEAF, LEAF), bf16),
        pltpu.VMEM((LEAVES, RANK, LEAF), bf16),
        pltpu.VMEM((NODES, RANK, RANK), bf16),
        pltpu.VMEM((16, RANK, 2 * RANK), bf16),
        pltpu.VMEM((NODES, RANK, 4 * RANK), bf16),
        pltpu.VMEM((NODES, RANK, COLS), bf16),
        pltpu.VMEM((NODES, RANK, COLS), f32),
        pltpu.VMEM((DEV, RANK, COLS), bf16),
        pltpu.VMEM((DEV, RANK, COLS), bf16),
        pltpu.VMEM((DEV, RANK, COLS), bf16),
        pltpu.VMEM((1, COLS), i32),
        pltpu.VMEM((DEV, 1, COLS), i32),
        pltpu.VMEM((8, DEV), i32),
        pltpu.SMEM((8, DEV), i32),
        pltpu.VMEM((RANK, RANK), bf16),
        pltpu.VMEM((2, RANK, COLS), bf16),
        pltpu.VMEM((2, 4, 16, COLS), bf16),
        pltpu.VMEM((64, 16, COLS), bf16),
        pltpu.VMEM((64, 16, COLS), bf16),
        pltpu.VMEM((COARSE, RANK, COLS), bf16),
        pltpu.VMEM((RANK, RANK, COARSE - 2), bf16),
        pltpu.VMEM(((RANK + 1) * (COARSE - 2), RANK), f32),
        pltpu.VMEM((COARSE - 2, RANK, RANK), bf16),
        pltpu.VMEM((62, RANK, 2 * RANK), bf16),
        pltpu.VMEM((10, RANK, 4 * RANK), bf16),
        pltpu.VMEM((2, 4, 16, COLS), bf16),
        pltpu.VMEM((2, 4, 16, COLS), bf16),
        dma((10,)),
        dma((7,)),
        dma((2,)),
        dma((2, 2)),
        dma((2, 2)),
        dma((3, 2)),
        dma((2,)),
        dma((2,)),
        dma((2,)),
        dma((2,)),
        dma((2,)),
        dma((2,)),
        dma(()),
    ]
    parts = pl.pallas_call(
        kernel,
        out_shape=(
            pltpu.VMEM((points, COLS), f32),
            pltpu.VMEM((points, COLS), f32),
            pltpu.VMEM((NODES, RANK, COLS), bf16),
            pltpu.VMEM((LEAVES, LEAF, RANK), bf16),
        ),
        in_specs=[hbm] * 11,
        out_specs=(vmem, vmem, vmem, vmem),
        scratch_shapes=scratch,
        compiler_params=pltpu.CompilerParams(
            collective_id=0, has_side_effects=True, vmem_limit_bytes=58 << 20
        ),
    )(
        sources.T,
        near_ids.T,
        coarse_sources.T,
        labels.reshape(points // COLS, COLS),
        weights,
        basis,
        near_tiles,
        transfer,
        couplings,
        coarse_transfer.transpose(1, 2, 0),
        coarse_couplings,
    )
    return pl.pallas_call(
        last_kernel,
        out_shape=(
            jax.ShapeDtypeStruct((points, COLS), f32),
            jax.ShapeDtypeStruct((points, COLS), f32),
        ),
        in_specs=[vmem] * 4,
        out_specs=(hbm, hbm),
        scratch_shapes=[
            pltpu.VMEM((points, COLS), f32),
            pltpu.VMEM((points, COLS), f32),
            dma((2, 4)),
        ],
        compiler_params=pltpu.CompilerParams(vmem_limit_bytes=16 << 20),
    )(*parts)


def solution(mesh):
    in_specs = (
        P("leaf", None),
        P("leaf"),
        P("leaf", None, None),
        P("leaf", None, None, None),
        P("leaf", None),
        P("leaf", None, None),
        P("leaf", None, None),
        P("leaf", None),
        P(),
        P(),
        P(),
    )
    out_specs = (P("leaf", None), P("leaf", None))
    return jax.shard_map(local, mesh=mesh, in_specs=in_specs, out_specs=out_specs, check_vma=False)
```

```python
import functools

import jax
import jax.numpy as jnp
from jax import lax
from jax.experimental import pallas as pl
from jax.experimental.pallas import tpu as pltpu
from jax.sharding import PartitionSpec as P

MESH = pl.DeviceIdType.MESH
DEV = 128
LEAVES = 16
LEAF = 256
RANK = 64
NODES = 31
COLS = 128
HALO = 2
COARSE = 126
STARTS = (0, 16, 24, 28, 30)
COARSE_AT = (0, 64, 96, 112, 120, 124)
BATCH = 8
BATCHES = DEV // BATCH


def mm(a, b):
    return jnp.dot(a, b, preferred_element_type=jnp.float32)


def pack(wide, turn):
    group = lax.div(lax.broadcasted_iota(jnp.int32, (16, COLS), 1), 32)
    out = wide[0:16]
    if turn % 4:
        out = pltpu.roll(out, 32 * (turn % 4), 1)
    for g in range(1, 4):
        part = wide[16 * g : 16 * g + 16]
        by = (g + turn) % 4
        if by:
            part = pltpu.roll(part, 32 * by, 1)
        out = jnp.where(group == g, part, out)
    return out.astype(jnp.bfloat16)


def unpack(ref, node):
    part = ref[node].astype(jnp.float32)
    parts = [part] + [pltpu.roll(part, 32 * (4 - g), 1) for g in range(1, 4)]
    return jnp.concatenate(parts, axis=0).astype(jnp.bfloat16)


def join(ref, phase):
    group = lax.div(lax.broadcasted_iota(jnp.int32, (16, COLS), 1), 32)
    parts = [ref[phase, v].astype(jnp.float32) for v in range(4)]
    rows = []
    for g in range(4):
        row = parts[0]
        if g:
            row = pltpu.roll(row, 32 * (4 - g), 1)
        for v in range(1, 4):
            by = (v - g) % 4
            part = pltpu.roll(parts[v], 32 * by, 1) if by else parts[v]
            row = jnp.where(group == v, part, row)
        rows.append(row)
    return jnp.concatenate(rows, axis=0).astype(jnp.bfloat16)


def within(i, count):
    return lax.max(lax.min(i, count - 1), 0)


def coords(me):
    return (
        lax.div(me, 32),
        lax.rem(lax.div(me, 8), 4),
        lax.rem(lax.div(me, 2), 4),
        lax.rem(me, 2),
    )


def batch_of(me, b):
    x, y, z, c = coords(me)
    bx, by = lax.div(b, 4), lax.rem(b, 4)
    xs = [lax.rem(x + bx + j, 4) * 32 for j in range(4)]
    ys = [lax.rem(y + by + j, 4) * 8 for j in range(4)]
    zs = [lax.rem(z + j, 4) * 2 for j in range(4)]
    cs = [c, 1 - c]
    return [
        xs[j] + ys[(j + 2 * k) % 4] + zs[j] + cs[k] for j in range(4) for k in range(2)
    ]


def far_first(me, act):
    x, y, z, c = coords(me)
    xs = [lax.rem(x + j, 4) * 32 for j in range(4)]
    ys = [lax.rem(y + j, 4) * 8 for j in range(4)]
    zs = [lax.rem(z + j, 4) * 2 for j in range(4)]
    cs = [c, 1 - c]
    hops = (0, 1, 2, 1)
    order = sorted(range(1, DEV), key=lambda k: -sum(hops[k >> s & 3] for s in (1, 3, 5)))
    for k in order:
        act(xs[k >> 5] + ys[k >> 3 & 3] + zs[k >> 1 & 3] + cs[k & 1])


def for_some(me, act, lo, hi):
    if lo == 0:
        for device in batch_of(me, 0)[1:]:
            act(device)
        lo = 1

    def one(b, carry):
        for device in batch_of(me, b):
            act(device)
        return carry

    lax.fori_loop(lo, hi, one, 0)


def remote(src, dst, send_sem, recv_sem, device):
    return pltpu.make_async_remote_copy(
        src_ref=src,
        dst_ref=dst,
        send_sem=send_sem,
        recv_sem=recv_sem,
        device_id=(device,),
        device_id_type=MESH,
    )


def take(ref, sem):
    pltpu.make_async_copy(ref, ref, sem).wait()


def kernel(
    sources_h,
    near_ids_h,
    coarse_sources_h,
    labels_h,
    weights_h,
    basis_h,
    near_h,
    transfer_h,
    couplings_h,
    coarse_transfer_h,
    coarse_couplings_h,
    based,
    acc,
    field,
    basis_t,
    sources_s,
    near_ids_s,
    coarse_sources_s,
    sources_v,
    labels_v,
    w,
    shift,
    vals0,
    vals1,
    halo0,
    halo1,
    near,
    basis,
    maps,
    maps_t,
    blocks,
    coef,
    coupled,
    send,
    recv0,
    recv1,
    request,
    requests,
    chosen_v,
    chosen,
    mate_map,
    mate_coef,
    own_coarse,
    packed0,
    packed1,
    table,
    planes_in,
    planes,
    cmaps,
    cmaps_t,
    cblocks,
    f1_out,
    f1_in,
    in_sem,
    coarse_sem,
    list_sem,
    halo_send,
    halo_recv,
    mate_sem,
    gather_send,
    gather_recv,
    block_send,
    block_recv,
    f1_send,
    f1_recv,
    small_sem,
):
    me = lax.axis_index("leaf")
    vals, recv, packed = (vals0, vals1), (recv0, recv1), (packed0, packed1)
    halo = (halo0, halo1)
    x, y, z, c = coords(me)
    line = x * 4 + y
    mate = me + 1 - 2 * c
    is_server = c == 1 - lax.rem(y, 2)

    barrier = pltpu.get_barrier_semaphore()

    def greet(device):
        pl.semaphore_signal(
            barrier, inc=1, device_id=(device,), device_id_type=MESH
        )

    loads = [
        pltpu.make_async_copy(src, dst, in_sem.at[i])
        for i, (src, dst) in enumerate(
            (
                (sources_h, sources_v),
                (weights_h, w),
                (basis_h, basis),
                (transfer_h, maps),
                (couplings_h, blocks),
                (sources_h, sources_s),
                (near_ids_h, near_ids_s),
                (coarse_sources_h, coarse_sources_s),
                (labels_h, labels_v),
                (near_h, near),
            )
        )
    ]
    for load in loads:
        load.start()
    far_first(me, greet)

    coarse_rows = (
        (0, 4 * line, 4),
        (4, 64 + 2 * line, 2),
        (6, 96 + line, 1),
        (7, 112 + lax.div(line, 2), 1),
        (8, 120 + lax.div(line, 4), 1),
        (9, 124 + lax.div(line, 8), 1),
    )
    coarse_loads = [
        pltpu.make_async_copy(coarse_transfer_h, planes_in, coarse_sem.at[6])
    ] + [
        pltpu.make_async_copy(
            coarse_couplings_h.at[pl.ds(row, count)],
            cblocks.at[pl.ds(at, count)],
            coarse_sem.at[i],
        )
        for i, (at, row, count) in enumerate(coarse_rows)
    ]

    @pl.when(is_server)
    def _():
        for load in coarse_loads:
            load.start()

    node = lax.broadcasted_iota(jnp.int32, (4, NODES), 1)
    bits = jnp.full((4, NODES), 4, jnp.int32)
    first = jnp.zeros((4, NODES), jnp.int32)
    for height in range(1, 5):
        bits = jnp.where(node >= STARTS[height], 4 - height, bits)
        first = jnp.where(node >= STARTS[height], STARTS[height], first)
    loads[0].wait()
    name = sources_v[...]
    owner = lax.shift_right_logical(name, bits)
    row = first + name - lax.shift_left(owner, bits)
    pad = jnp.zeros((4, COLS - NODES), jnp.int32)
    owner = jnp.concatenate([owner, pad], axis=1).astype(jnp.float32)
    row = jnp.concatenate([row, pad], axis=1).astype(jnp.float32)
    device = lax.broadcasted_iota(jnp.int32, (COLS, COLS), 0)
    hits = jnp.zeros((8, COLS), jnp.float32)
    for k in range(4):
        at = jnp.broadcast_to(owner[k : k + 1], (COLS, COLS)).astype(jnp.int32)
        hot = (at == device).astype(jnp.float32).astype(jnp.bfloat16)
        rows = jnp.broadcast_to(row[k : k + 1], (8, COLS)).astype(jnp.bfloat16)
        hits += lax.dot_general(
            rows, hot, (((1,), (1,)), ((), ())), preferred_element_type=jnp.float32
        )
    asked = hits[0:1].astype(jnp.int32)
    request[...] = asked
    requests[pl.ds(me, 1)] = asked.reshape(1, 1, COLS)

    def half_round(t, carry):
        rows = pl.ds(pl.multiple_of(t * LEAF, LEAF), LEAF)
        v = w[rows, :].astype(jnp.bfloat16)
        vals0[t] = v
        coef[t] = mm(basis[t], v).astype(jnp.bfloat16)
        return carry

    def climb():
        for height in range(4):
            for j in range(LEAVES >> (height + 1)):
                lo = STARTS[height] + 2 * j
                up = STARTS[height + 1] + j
                kids = coef[lo : lo + 2].reshape(2 * RANK, COLS)
                coef[up] = mm(maps_t[up - LEAVES], kids).astype(jnp.bfloat16)

    loads[1].wait()
    loads[2].wait()
    lax.fori_loop(0, LEAVES, half_round, 0, unroll=4)
    loads[3].wait()

    def turn(j, carry):
        lo = 2 * j
        pair = maps[pl.ds(lo, 2)].reshape(2 * RANK, RANK)
        maps_t[j] = pair.astype(jnp.float32).T.astype(jnp.bfloat16)
        return carry

    lax.fori_loop(0, 15, turn, 0, unroll=5)
    climb()

    def turn_basis(t, carry):
        basis_t[t] = basis[t].astype(jnp.float32).T.astype(jnp.bfloat16)
        return carry

    lane = lax.broadcasted_iota(jnp.int32, (COLS, COLS), 1)

    def mark(i, carry):
        rows = pl.ds(pl.multiple_of(i * COLS, COLS), COLS)
        row = jnp.broadcast_to(labels_v[pl.ds(i, 1), :], (COLS, COLS))
        column = row.astype(jnp.float32).T.astype(jnp.int32)
        shift[rows, :] = jnp.where(column == lane, 0.25, -0.25).astype(jnp.bfloat16)
        return carry

    for load in loads[4:9]:
        load.wait()
    pl.semaphore_wait(barrier, DEV - 1)

    def halo_copies(phase):
        after = lax.rem(me + 1, DEV)
        before = lax.rem(me + DEV - 1, DEV)
        v = vals[phase]
        return (
            remote(
                v.at[pl.ds(LEAVES - HALO, HALO)],
                halo[phase].at[pl.ds(0, HALO)],
                halo_send.at[phase, 0],
                halo_recv.at[phase, 0],
                after,
            ),
            remote(
                v.at[pl.ds(0, HALO)],
                halo[phase].at[pl.ds(HALO, HALO)],
                halo_send.at[phase, 1],
                halo_recv.at[phase, 1],
                before,
            ),
        )

    def gather_copies(phase, i):
        to_line = 2 * i + c
        for v in range(4):
            remote(
                own_coarse.at[phase, v],
                packed[phase].at[lax.div(me, 2)],
                gather_send.at[phase],
                gather_recv.at[phase],
                (to_line * 4 + v) * 2 + 1 - c,
            ).start()

    def mate_copy(phase):
        return remote(
            coef.at[NODES - 1],
            mate_coef.at[phase],
            mate_sem.at[phase, 0],
            mate_sem.at[phase, 1],
            mate,
        )

    map_copy = remote(
        maps.at[NODES - 1], mate_map, mate_sem.at[2, 0], mate_sem.at[2, 1], mate
    )

    def list_copy(device):
        remote(
            request, requests.at[me], list_sem.at[0], list_sem.at[1], device
        ).start()

    def block_copy(phase, device):
        remote(
            send.at[device],
            recv[phase].at[me],
            block_send.at[phase],
            block_recv.at[phase],
            device,
        ).start()

    def send_top(phase):
        mate_copy(phase).wait_recv()
        if phase == 0:
            map_copy.wait_recv()
            pair = jnp.concatenate(
                [
                    jnp.where(c == 0, maps[NODES - 1].astype(jnp.float32), mate_map[...].astype(jnp.float32)),
                    jnp.where(c == 0, mate_map[...].astype(jnp.float32), maps[NODES - 1].astype(jnp.float32)),
                ],
                axis=0,
            )
            maps_t[15] = pair.T.astype(jnp.bfloat16)
        mine = coef[NODES - 1].astype(jnp.float32)
        theirs = mate_coef[phase].astype(jnp.float32)
        kids = jnp.concatenate(
            [jnp.where(c == 0, mine, theirs), jnp.where(c == 0, theirs, mine)], axis=0
        ).astype(jnp.bfloat16)
        made = mm(maps_t[15], kids)
        for v in range(4):
            own_coarse[phase, v] = pack(made, -v)

        def spread(i, carry):
            gather_copies(phase, i)
            return carry

        lax.fori_loop(0, 8, spread, 0)

    def fill(lo, hi):
        def one(d, carry):
            send[d] = coef[within(chosen[0, d], NODES)]
            return carry

        lax.fori_loop(lo, hi, one, 0, unroll=8)

    def near_leaf(phase, t, edge):
        rows = pl.ds(pl.multiple_of(t * LEAF, LEAF), LEAF)
        total = mm(near[t, 0], vals[phase][t])
        for i in range(2):
            at = near_ids_s[i, t] - me * LEAVES
            v = vals[phase][within(at, LEAVES)]
            if edge:
                inside = (at >= 0) & (at < LEAVES)
                slot = jnp.where(at < 0, at + HALO, at + HALO - LEAVES)
                far = halo[phase][within(slot, 2 * HALO)]
                v = jnp.where(inside, v, far)
            total += mm(near[t, i + 1], v)
        acc[rows, :] = total

    def send_blocks(phase, lo, hi):
        for_some(me, lambda device: block_copy(phase, device), lo, hi)

    def blocks_sent(phase):
        take(send.at[pl.ds(0, DEV - 1)], block_send.at[phase])

    def prepare_server():
        for load in coarse_loads:
            load.wait()

        def flip(i, carry):
            plane = planes_in[i].astype(jnp.float32).T
            rows = pl.ds(pl.multiple_of(i * (COARSE - 2), 4), COARSE - 2)
            planes[rows, :] = plane
            return carry

        lax.fori_loop(0, RANK, flip, 0, unroll=4)

        def turn_coarse(j, carry):
            for n in (2 * j, 2 * j + 1):
                one = planes[pl.ds(n, RANK, stride=COARSE - 2), :]
                cmaps[n] = one.astype(jnp.bfloat16)
            pair = cmaps[pl.ds(2 * j, 2)].reshape(2 * RANK, RANK)
            cmaps_t[j] = pair.astype(jnp.float32).T.astype(jnp.bfloat16)
            return carry

        lax.fori_loop(0, 62, turn_coarse, 0, unroll=2)

    def serve(phase):
        take(packed[phase], gather_recv.at[phase])

        def open_up(n, carry):
            table[n] = unpack(packed[phase], n)
            return carry

        lax.fori_loop(0, 64, open_up, 0, unroll=8)
        for level in range(5):
            at, above = COARSE_AT[level], COARSE_AT[level + 1]

            group = min(32 >> level, 8)
            for j in range(0, 32 >> level, group):
                made = [
                    mm(
                        cmaps_t[at // 2 + i],
                        table[at + 2 * i : at + 2 * i + 2].reshape(2 * RANK, COLS),
                    ).astype(jnp.bfloat16)
                    for i in range(j, j + group)
                ]
                for i in range(group):
                    table[above + j + i] = made[i]

        def term(slot, level, row):
            at = COARSE_AT[level]
            kids = jnp.concatenate(
                [table[at + within(coarse_sources_s[k, row], DEV >> (level + 1))] for k in range(4)], axis=0
            )
            return mm(cblocks[slot], kids)

        rows = [row for _, row, _ in coarse_rows]
        terms = [
            term(slot, level, rows[level] + i)
            for level, (at, _, count) in enumerate(coarse_rows)
            for i, slot in enumerate(range(at, at + count))
        ]
        f = terms[9].astype(jnp.bfloat16)
        for slot, level in ((8, 4), (7, 3), (6, 2)):
            f = (terms[slot] + mm(cmaps[rows[level]], f)).astype(jnp.bfloat16)
        for i in range(2):
            g = (terms[4 + i] + mm(cmaps[rows[1] + i], f)).astype(jnp.bfloat16)
            for j in range(2):
                n = 2 * i + j
                whole = terms[n] + mm(cmaps[rows[0] + n], g)
                f1_out[phase, n] = pack(whole, 0)
        for o in range(1, 8):
            f1_copy(phase, o).start()
        f1_in[phase, z] = f1_out[phase, z]

    def f1_copy(phase, o):
        tz = lax.rem(z + o // 2, 4)
        to = (line * 4 + tz) * 2 + lax.rem(c + o % 2, 2)
        return remote(
            f1_out.at[phase, tz],
            f1_in.at[phase, z],
            f1_send.at[phase],
            f1_recv.at[phase],
            to,
        )

    def exchange(phase):
        if phase == 0:
            lax.fori_loop(0, LEAVES, turn_basis, 0, unroll=4)
            lax.fori_loop(0, LEAVES * LEAF // COLS, mark, 0, unroll=4)

        if phase == 0:
            loads[9].wait()

            @pl.when(is_server)
            def _():
                serve(phase)


        def pair(t, carry):
            near_leaf(phase, 2 * t, False)
            near_leaf(phase, 2 * t + 1, False)
            return carry

        lax.fori_loop(1, LEAVES // 2 - 1, pair, 0)
        for h in halo_copies(phase):
            h.wait_recv()

        def edge_pair(i, carry):
            near_leaf(phase, i * (LEAVES - HALO), True)
            near_leaf(phase, i * (LEAVES - HALO) + 1, True)
            return carry

        lax.fori_loop(0, 2, edge_pair, 0)
        if phase == 1:

            @pl.when(is_server)
            def _():
                serve(phase)

    def finish(phase):
        take(recv[phase].at[pl.ds(0, DEV - 1)], block_recv.at[phase])

        def couple(t, bits):
            kids = jnp.concatenate(
                [
                    recv[phase][within(lax.shift_right_logical(sources_s[k, t], bits), DEV)]
                    for k in range(4)
                ],
                axis=0,
            )
            coupled[t] = mm(blocks[t], kids)

        def leaf_pair(t, carry):
            couple(t, 4)
            return carry

        for t in range(NODES - 1, LEAVES - 1, -1):
            height = max(h for h in range(5) if t >= STARTS[h])
            couple(t, 4 - height)
        lax.fori_loop(0, LEAVES, leaf_pair, 0, unroll=4)

        @pl.when(jnp.logical_not(is_server))
        def _():
            take(f1_in.at[phase], f1_recv.at[phase])

        @pl.when(is_server)
        def _():
            take(f1_in.at[phase, pl.ds(0, 3)], f1_recv.at[phase])

        field[NODES - 1] = (
            coupled[NODES - 1] + mm(maps[NODES - 1], join(f1_in, phase))
        ).astype(jnp.bfloat16)
        for height in range(3, -1, -1):
            for j in range(LEAVES >> (height + 1)):
                lo = STARTS[height] + 2 * j
                pushed = mm(
                    maps[lo : lo + 2].reshape(2 * RANK, RANK),
                    field[STARTS[height + 1] + j],
                )
                both = coupled[lo : lo + 2] + pushed.reshape(2, RANK, COLS)
                field[lo : lo + 2] = both.astype(jnp.bfloat16)

    def first_leaf(t, carry):
        rows = pl.ds(pl.multiple_of(t * LEAF, LEAF), LEAF)
        score = acc[rows, :] + mm(basis_t[t], field[t])
        marked = shift[rows, :].astype(jnp.float32)
        middle = w[rows, :] + (marked - 0.25 * jnp.tanh(0.5 * score))
        based[rows, :] = middle + marked
        v = middle.astype(jnp.bfloat16)
        vals1[t] = v
        return carry

    def second_coef(t, carry):
        coef[t] = mm(basis[t], vals1[t]).astype(jnp.bfloat16)
        return carry

    map_copy.start()
    mate_copy(0).start()

    far_first(me, list_copy)

    @pl.when(is_server)
    def _():
        prepare_server()

    take(requests.at[pl.ds(0, DEV - 1)], list_sem.at[1])
    mine = (lax.broadcasted_iota(jnp.int32, (8, DEV), 1) == me).astype(jnp.bfloat16)
    asks = requests[...].reshape(DEV, COLS).astype(jnp.float32).astype(jnp.bfloat16)
    wanted = lax.dot_general(
        mine, asks, (((1,), (1,)), ((), ())), preferred_element_type=jnp.float32
    )
    chosen_v[...] = jnp.clip(wanted, 0, NODES - 1).astype(jnp.int32)
    small = pltpu.make_async_copy(chosen_v, chosen, small_sem)
    small.start()
    send_top(0)
    small.wait()
    fill(0, DEV)
    recv0[me] = coef[within(chosen[0, me], NODES)]
    send_blocks(0, 0, 8)
    for h in halo_copies(0):
        h.start()
    send_blocks(0, 8, BATCHES)
    exchange(0)
    finish(0)
    lax.fori_loop(0, LEAVES, first_leaf, 0, unroll=4)
    for h in halo_copies(1):
        h.start()
    lax.fori_loop(0, LEAVES, second_coef, 0, unroll=4)

    blocks_sent(0)
    mate_copy(0).wait_send()
    climb()
    mate_copy(1).start()
    fill(0, DEV)
    recv1[me] = coef[within(chosen[0, me], NODES)]
    send_blocks(1, 0, 2)
    send_top(1)
    send_blocks(1, 2, BATCHES)
    exchange(1)
    finish(1)

    map_copy.wait_send()
    take(requests.at[pl.ds(0, DEV - 1)], list_sem.at[0])
    mate_copy(1).wait_send()
    blocks_sent(1)
    for phase in range(2):
        for h in halo_copies(phase):
            h.wait_send()
        take(packed[phase].at[pl.ds(0, 32)], gather_send.at[phase])

        @pl.when(is_server)
        def _():
            take(packed[phase].at[pl.ds(0, 7)], f1_send.at[phase])


def last_kernel(based, near_term, field, basis_t, updated_h, scores_h, updated, scores, sem):
    copies = []
    for part in range(4):
        for t in range(4 * part, 4 * part + 4):
            rows = pl.ds(t * LEAF, LEAF)
            score = near_term[rows, :] + mm(basis_t[t], field[t])
            scores[rows, :] = score
            updated[rows, :] = based[rows, :] - 0.25 * jnp.tanh(0.5 * score)
        rows = pl.ds(4 * part * LEAF, 4 * LEAF)
        for i, (src, dst) in enumerate(((updated, updated_h), (scores, scores_h))):
            copies.append(
                pltpu.make_async_copy(src.at[rows], dst.at[rows], sem.at[i, part])
            )
            copies[-1].start()
    for copy in copies:
        copy.wait()


def local(
    weights,
    labels,
    basis,
    near_tiles,
    near_ids,
    transfer,
    couplings,
    sources,
    coarse_transfer,
    coarse_couplings,
    coarse_sources,
):
    bf16, f32, i32 = jnp.bfloat16, jnp.float32, jnp.int32
    points = LEAVES * LEAF
    vmem = pl.BlockSpec(memory_space=pltpu.VMEM)
    hbm = pl.BlockSpec(memory_space=pl.ANY)
    dma = pltpu.SemaphoreType.DMA
    scratch = [
        pltpu.SMEM((4, NODES), i32),
        pltpu.SMEM((2, LEAVES), i32),
        pltpu.SMEM((4, COARSE), i32),
        pltpu.VMEM((4, NODES), i32),
        pltpu.VMEM((points // COLS, COLS), i32),
        pltpu.VMEM((points, COLS), f32),
        pltpu.VMEM((points, COLS), bf16),
        pltpu.VMEM((LEAVES, LEAF, COLS), bf16),
        pltpu.VMEM((LEAVES, LEAF, COLS), bf16),
        pltpu.VMEM((2 * HALO, LEAF, COLS), bf16),
        pltpu.VMEM((2 * HALO, LEAF, COLS), bf16),
        pltpu.VMEM((LEAVES, 3, LEAF, LEAF), bf16),
        pltpu.VMEM((LEAVES, RANK, LEAF), bf16),
        pltpu.VMEM((NODES, RANK, RANK), bf16),
        pltpu.VMEM((16, RANK, 2 * RANK), bf16),
        pltpu.VMEM((NODES, RANK, 4 * RANK), bf16),
        pltpu.VMEM((NODES, RANK, COLS), bf16),
        pltpu.VMEM((NODES, RANK, COLS), f32),
        pltpu.VMEM((DEV, RANK, COLS), bf16),
        pltpu.VMEM((DEV, RANK, COLS), bf16),
        pltpu.VMEM((DEV, RANK, COLS), bf16),
        pltpu.VMEM((1, COLS), i32),
        pltpu.VMEM((DEV, 1, COLS), i32),
        pltpu.VMEM((8, DEV), i32),
        pltpu.SMEM((8, DEV), i32),
        pltpu.VMEM((RANK, RANK), bf16),
        pltpu.VMEM((2, RANK, COLS), bf16),
        pltpu.VMEM((2, 4, 16, COLS), bf16),
        pltpu.VMEM((64, 16, COLS), bf16),
        pltpu.VMEM((64, 16, COLS), bf16),
        pltpu.VMEM((COARSE, RANK, COLS), bf16),
        pltpu.VMEM((RANK, RANK, COARSE - 2), bf16),
        pltpu.VMEM(((RANK + 1) * (COARSE - 2), RANK), f32),
        pltpu.VMEM((COARSE - 2, RANK, RANK), bf16),
        pltpu.VMEM((62, RANK, 2 * RANK), bf16),
        pltpu.VMEM((10, RANK, 4 * RANK), bf16),
        pltpu.VMEM((2, 4, 16, COLS), bf16),
        pltpu.VMEM((2, 4, 16, COLS), bf16),
        dma((10,)),
        dma((7,)),
        dma((2,)),
        dma((2, 2)),
        dma((2, 2)),
        dma((3, 2)),
        dma((2,)),
        dma((2,)),
        dma((2,)),
        dma((2,)),
        dma((2,)),
        dma((2,)),
        dma(()),
    ]
    parts = pl.pallas_call(
        kernel,
        out_shape=(
            pltpu.VMEM((points, COLS), f32),
            pltpu.VMEM((points, COLS), f32),
            pltpu.VMEM((NODES, RANK, COLS), bf16),
            pltpu.VMEM((LEAVES, LEAF, RANK), bf16),
        ),
        in_specs=[hbm] * 11,
        out_specs=(vmem, vmem, vmem, vmem),
        scratch_shapes=scratch,
        compiler_params=pltpu.CompilerParams(
            collective_id=0, has_side_effects=True, vmem_limit_bytes=58 << 20
        ),
    )(
        sources.T,
        near_ids.T,
        coarse_sources.T,
        labels.reshape(points // COLS, COLS),
        weights,
        basis,
        near_tiles,
        transfer,
        couplings,
        coarse_transfer.transpose(1, 2, 0),
        coarse_couplings,
    )
    return pl.pallas_call(
        last_kernel,
        out_shape=(
            jax.ShapeDtypeStruct((points, COLS), f32),
            jax.ShapeDtypeStruct((points, COLS), f32),
        ),
        in_specs=[vmem] * 4,
        out_specs=(hbm, hbm),
        scratch_shapes=[
            pltpu.VMEM((points, COLS), f32),
            pltpu.VMEM((points, COLS), f32),
            dma((2, 4)),
        ],
        compiler_params=pltpu.CompilerParams(vmem_limit_bytes=16 << 20),
    )(*parts)


def solution(mesh):
    in_specs = (
        P("leaf", None),
        P("leaf"),
        P("leaf", None, None),
        P("leaf", None, None, None),
        P("leaf", None),
        P("leaf", None, None),
        P("leaf", None, None),
        P("leaf", None),
        P(),
        P(),
        P(),
    )
    out_specs = (P("leaf", None), P("leaf", None))
    return jax.shard_map(local, mesh=mesh, in_specs=in_specs, out_specs=out_specs, check_vma=False)
```

```python
import functools

import jax
import jax.numpy as jnp
from jax import lax
from jax.experimental import pallas as pl
from jax.experimental.pallas import tpu as pltpu
from jax.sharding import PartitionSpec as P

MESH = pl.DeviceIdType.MESH
DEV = 128
LEAVES = 16
LEAF = 256
RANK = 64
NODES = 31
COLS = 128
HALO = 2
COARSE = 126
STARTS = (0, 16, 24, 28, 30)
COARSE_AT = (0, 64, 96, 112, 120, 124)
BATCH = 8
BATCHES = DEV // BATCH


def mm(a, b):
    return jnp.dot(a, b, preferred_element_type=jnp.float32)


def pack(wide, turn):
    group = lax.div(lax.broadcasted_iota(jnp.int32, (16, COLS), 1), 32)
    out = wide[0:16]
    if turn % 4:
        out = pltpu.roll(out, 32 * (turn % 4), 1)
    for g in range(1, 4):
        part = wide[16 * g : 16 * g + 16]
        by = (g + turn) % 4
        if by:
            part = pltpu.roll(part, 32 * by, 1)
        out = jnp.where(group == g, part, out)
    return out.astype(jnp.bfloat16)


def unpack(ref, node):
    part = ref[node].astype(jnp.float32)
    parts = [part] + [pltpu.roll(part, 32 * (4 - g), 1) for g in range(1, 4)]
    return jnp.concatenate(parts, axis=0).astype(jnp.bfloat16)


def join(ref, phase):
    group = lax.div(lax.broadcasted_iota(jnp.int32, (16, COLS), 1), 32)
    parts = [ref[phase, v].astype(jnp.float32) for v in range(4)]
    rows = []
    for g in range(4):
        row = parts[0]
        if g:
            row = pltpu.roll(row, 32 * (4 - g), 1)
        for v in range(1, 4):
            by = (v - g) % 4
            part = pltpu.roll(parts[v], 32 * by, 1) if by else parts[v]
            row = jnp.where(group == v, part, row)
        rows.append(row)
    return jnp.concatenate(rows, axis=0).astype(jnp.bfloat16)


def within(i, count):
    return lax.max(lax.min(i, count - 1), 0)


def coords(me):
    return (
        lax.div(me, 32),
        lax.rem(lax.div(me, 8), 4),
        lax.rem(lax.div(me, 2), 4),
        lax.rem(me, 2),
    )


def batch_of(me, b):
    x, y, z, c = coords(me)
    bx, by = lax.div(b, 4), lax.rem(b, 4)
    xs = [lax.rem(x + bx + j, 4) * 32 for j in range(4)]
    ys = [lax.rem(y + by + j, 4) * 8 for j in range(4)]
    zs = [lax.rem(z + j, 4) * 2 for j in range(4)]
    cs = [c, 1 - c]
    return [
        xs[j] + ys[(j + 2 * k) % 4] + zs[j] + cs[k] for j in range(4) for k in range(2)
    ]


def far_first(me, act):
    x, y, z, c = coords(me)
    xs = [lax.rem(x + j, 4) * 32 for j in range(4)]
    ys = [lax.rem(y + j, 4) * 8 for j in range(4)]
    zs = [lax.rem(z + j, 4) * 2 for j in range(4)]
    cs = [c, 1 - c]
    hops = (0, 1, 2, 1)
    order = sorted(range(1, DEV), key=lambda k: -sum(hops[k >> s & 3] for s in (1, 3, 5)))
    for k in order:
        act(xs[k >> 5] + ys[k >> 3 & 3] + zs[k >> 1 & 3] + cs[k & 1])


def for_some(me, act, lo, hi):
    if lo == 0:
        for device in batch_of(me, 0)[1:]:
            act(device)
        lo = 1

    def one(b, carry):
        for device in batch_of(me, b):
            act(device)
        return carry

    lax.fori_loop(lo, hi, one, 0)


def remote(src, dst, send_sem, recv_sem, device):
    return pltpu.make_async_remote_copy(
        src_ref=src,
        dst_ref=dst,
        send_sem=send_sem,
        recv_sem=recv_sem,
        device_id=(device,),
        device_id_type=MESH,
    )


def take(ref, sem):
    pltpu.make_async_copy(ref, ref, sem).wait()


def kernel(
    sources_h,
    near_ids_h,
    coarse_sources_h,
    labels_h,
    weights_h,
    basis_h,
    near_h,
    transfer_h,
    couplings_h,
    coarse_transfer_h,
    coarse_couplings_h,
    based,
    acc,
    field,
    basis_t,
    sources_s,
    near_ids_s,
    coarse_sources_s,
    sources_v,
    labels_v,
    w,
    shift,
    vals0,
    vals1,
    halo0,
    halo1,
    near,
    basis,
    maps,
    maps_t,
    blocks,
    coef,
    coupled,
    send,
    recv0,
    recv1,
    request,
    requests,
    chosen_v,
    chosen,
    mate_map,
    mate_coef,
    own_coarse,
    packed0,
    packed1,
    table,
    planes_in,
    planes,
    cmaps,
    cmaps_t,
    cblocks,
    f1_out,
    f1_in,
    in_sem,
    coarse_sem,
    list_sem,
    halo_send,
    halo_recv,
    mate_sem,
    gather_send,
    gather_recv,
    block_send,
    block_recv,
    f1_send,
    f1_recv,
    small_sem,
):
    me = lax.axis_index("leaf")
    vals, recv, packed = (vals0, vals1), (recv0, recv1), (packed0, packed1)
    halo = (halo0, halo1)
    x, y, z, c = coords(me)
    line = x * 4 + y
    mate = me + 1 - 2 * c
    is_server = c == 1 - lax.rem(y, 2)

    barrier = pltpu.get_barrier_semaphore()

    def greet(device):
        pl.semaphore_signal(
            barrier, inc=1, device_id=(device,), device_id_type=MESH
        )

    loads = [
        pltpu.make_async_copy(src, dst, in_sem.at[i])
        for i, (src, dst) in enumerate(
            (
                (sources_h, sources_v),
                (weights_h, w),
                (basis_h, basis),
                (transfer_h, maps),
                (couplings_h, blocks),
                (sources_h, sources_s),
                (near_ids_h, near_ids_s),
                (coarse_sources_h, coarse_sources_s),
                (labels_h, labels_v),
                (near_h, near),
            )
        )
    ]
    for load in loads:
        load.start()
    far_first(me, greet)

    coarse_rows = (
        (0, 4 * line, 4),
        (4, 64 + 2 * line, 2),
        (6, 96 + line, 1),
        (7, 112 + lax.div(line, 2), 1),
        (8, 120 + lax.div(line, 4), 1),
        (9, 124 + lax.div(line, 8), 1),
    )
    coarse_loads = [
        pltpu.make_async_copy(coarse_transfer_h, planes_in, coarse_sem.at[6])
    ] + [
        pltpu.make_async_copy(
            coarse_couplings_h.at[pl.ds(row, count)],
            cblocks.at[pl.ds(at, count)],
            coarse_sem.at[i],
        )
        for i, (at, row, count) in enumerate(coarse_rows)
    ]

    @pl.when(is_server)
    def _():
        for load in coarse_loads:
            load.start()

    node = lax.broadcasted_iota(jnp.int32, (4, NODES), 1)
    bits = jnp.full((4, NODES), 4, jnp.int32)
    first = jnp.zeros((4, NODES), jnp.int32)
    for height in range(1, 5):
        bits = jnp.where(node >= STARTS[height], 4 - height, bits)
        first = jnp.where(node >= STARTS[height], STARTS[height], first)
    loads[0].wait()
    name = sources_v[...]
    owner = lax.shift_right_logical(name, bits)
    row = first + name - lax.shift_left(owner, bits)
    pad = jnp.zeros((4, COLS - NODES), jnp.int32)
    owner = jnp.concatenate([owner, pad], axis=1).astype(jnp.float32)
    row = jnp.concatenate([row, pad], axis=1).astype(jnp.float32)
    device = lax.broadcasted_iota(jnp.int32, (COLS, COLS), 0)
    hits = jnp.zeros((8, COLS), jnp.float32)
    for k in range(4):
        at = jnp.broadcast_to(owner[k : k + 1], (COLS, COLS)).astype(jnp.int32)
        hot = (at == device).astype(jnp.float32).astype(jnp.bfloat16)
        rows = jnp.broadcast_to(row[k : k + 1], (8, COLS)).astype(jnp.bfloat16)
        hits += lax.dot_general(
            rows, hot, (((1,), (1,)), ((), ())), preferred_element_type=jnp.float32
        )
    asked = hits[0:1].astype(jnp.int32)
    request[...] = asked
    requests[pl.ds(me, 1)] = asked.reshape(1, 1, COLS)

    def half_round(t, carry):
        rows = pl.ds(pl.multiple_of(t * LEAF, LEAF), LEAF)
        v = w[rows, :].astype(jnp.bfloat16)
        vals0[t] = v
        coef[t] = mm(basis[t], v).astype(jnp.bfloat16)
        return carry

    def climb():
        for height in range(4):
            for j in range(LEAVES >> (height + 1)):
                lo = STARTS[height] + 2 * j
                up = STARTS[height + 1] + j
                kids = coef[lo : lo + 2].reshape(2 * RANK, COLS)
                coef[up] = mm(maps_t[up - LEAVES], kids).astype(jnp.bfloat16)

    loads[1].wait()
    loads[2].wait()
    lax.fori_loop(0, LEAVES, half_round, 0, unroll=4)
    loads[3].wait()

    def turn(j, carry):
        lo = 2 * j
        pair = maps[pl.ds(lo, 2)].reshape(2 * RANK, RANK)
        maps_t[j] = pair.astype(jnp.float32).T.astype(jnp.bfloat16)
        return carry

    lax.fori_loop(0, 15, turn, 0, unroll=5)
    climb()

    def turn_basis(t, carry):
        basis_t[t] = basis[t].astype(jnp.float32).T.astype(jnp.bfloat16)
        return carry

    lane = lax.broadcasted_iota(jnp.int32, (COLS, COLS), 1)

    def mark(i, carry):
        rows = pl.ds(pl.multiple_of(i * COLS, COLS), COLS)
        row = jnp.broadcast_to(labels_v[pl.ds(i, 1), :], (COLS, COLS))
        column = row.astype(jnp.float32).T.astype(jnp.int32)
        shift[rows, :] = jnp.where(column == lane, 0.25, -0.25).astype(jnp.bfloat16)
        return carry

    for load in loads[4:9]:
        load.wait()
    pl.semaphore_wait(barrier, DEV - 1)

    def halo_copies(phase):
        after = lax.rem(me + 1, DEV)
        before = lax.rem(me + DEV - 1, DEV)
        v = vals[phase]
        return (
            remote(
                v.at[pl.ds(LEAVES - HALO, HALO)],
                halo[phase].at[pl.ds(0, HALO)],
                halo_send.at[phase, 0],
                halo_recv.at[phase, 0],
                after,
            ),
            remote(
                v.at[pl.ds(0, HALO)],
                halo[phase].at[pl.ds(HALO, HALO)],
                halo_send.at[phase, 1],
                halo_recv.at[phase, 1],
                before,
            ),
        )

    def gather_copies(phase, i):
        to_line = 2 * i + c
        for v in range(4):
            remote(
                own_coarse.at[phase, v],
                packed[phase].at[lax.div(me, 2)],
                gather_send.at[phase],
                gather_recv.at[phase],
                (to_line * 4 + v) * 2 + 1 - c,
            ).start()

    def mate_copy(phase):
        return remote(
            coef.at[NODES - 1],
            mate_coef.at[phase],
            mate_sem.at[phase, 0],
            mate_sem.at[phase, 1],
            mate,
        )

    map_copy = remote(
        maps.at[NODES - 1], mate_map, mate_sem.at[2, 0], mate_sem.at[2, 1], mate
    )

    def list_copy(device):
        remote(
            request, requests.at[me], list_sem.at[0], list_sem.at[1], device
        ).start()

    def block_copy(phase, device):
        remote(
            send.at[device],
            recv[phase].at[me],
            block_send.at[phase],
            block_recv.at[phase],
            device,
        ).start()

    def send_top(phase):
        mate_copy(phase).wait_recv()
        if phase == 0:
            map_copy.wait_recv()
            pair = jnp.concatenate(
                [
                    jnp.where(c == 0, maps[NODES - 1].astype(jnp.float32), mate_map[...].astype(jnp.float32)),
                    jnp.where(c == 0, mate_map[...].astype(jnp.float32), maps[NODES - 1].astype(jnp.float32)),
                ],
                axis=0,
            )
            maps_t[15] = pair.T.astype(jnp.bfloat16)
        mine = coef[NODES - 1].astype(jnp.float32)
        theirs = mate_coef[phase].astype(jnp.float32)
        kids = jnp.concatenate(
            [jnp.where(c == 0, mine, theirs), jnp.where(c == 0, theirs, mine)], axis=0
        ).astype(jnp.bfloat16)
        made = mm(maps_t[15], kids)
        for v in range(4):
            own_coarse[phase, v] = pack(made, -v)

        def spread(i, carry):
            gather_copies(phase, i)
            return carry

        lax.fori_loop(0, 8, spread, 0)

    def fill(lo, hi):
        def one(device):
            send[device] = coef[within(chosen[0, device], NODES)]

        for_some(me, one, lo, hi)

    def near_leaf(phase, t, edge):
        rows = pl.ds(pl.multiple_of(t * LEAF, LEAF), LEAF)
        total = mm(near[t, 0], vals[phase][t])
        for i in range(2):
            at = near_ids_s[i, t] - me * LEAVES
            v = vals[phase][within(at, LEAVES)]
            if edge:
                inside = (at >= 0) & (at < LEAVES)
                slot = jnp.where(at < 0, at + HALO, at + HALO - LEAVES)
                far = halo[phase][within(slot, 2 * HALO)]
                v = jnp.where(inside, v, far)
            total += mm(near[t, i + 1], v)
        acc[rows, :] = total

    def send_blocks(phase, lo, hi):
        for_some(me, lambda device: block_copy(phase, device), lo, hi)

    def blocks_sent(phase):
        take(send.at[pl.ds(0, DEV - 1)], block_send.at[phase])

    def prepare_server():
        for load in coarse_loads:
            load.wait()

        def flip(i, carry):
            plane = planes_in[i].astype(jnp.float32).T
            rows = pl.ds(pl.multiple_of(i * (COARSE - 2), 4), COARSE - 2)
            planes[rows, :] = plane
            return carry

        lax.fori_loop(0, RANK, flip, 0, unroll=4)

        def turn_coarse(j, carry):
            for n in (2 * j, 2 * j + 1):
                one = planes[pl.ds(n, RANK, stride=COARSE - 2), :]
                cmaps[n] = one.astype(jnp.bfloat16)
            pair = cmaps[pl.ds(2 * j, 2)].reshape(2 * RANK, RANK)
            cmaps_t[j] = pair.astype(jnp.float32).T.astype(jnp.bfloat16)
            return carry

        lax.fori_loop(0, 62, turn_coarse, 0, unroll=2)

    def serve(phase):
        take(packed[phase], gather_recv.at[phase])

        def open_up(n, carry):
            table[n] = unpack(packed[phase], n)
            return carry

        lax.fori_loop(0, 64, open_up, 0, unroll=8)
        for level in range(5):
            at, above = COARSE_AT[level], COARSE_AT[level + 1]

            group = min(32 >> level, 8)
            for j in range(0, 32 >> level, group):
                made = [
                    mm(
                        cmaps_t[at // 2 + i],
                        table[at + 2 * i : at + 2 * i + 2].reshape(2 * RANK, COLS),
                    ).astype(jnp.bfloat16)
                    for i in range(j, j + group)
                ]
                for i in range(group):
                    table[above + j + i] = made[i]

        def term(slot, level, row):
            at = COARSE_AT[level]
            kids = jnp.concatenate(
                [table[at + within(coarse_sources_s[k, row], DEV >> (level + 1))] for k in range(4)], axis=0
            )
            return mm(cblocks[slot], kids)

        rows = [row for _, row, _ in coarse_rows]
        terms = [
            term(slot, level, rows[level] + i)
            for level, (at, _, count) in enumerate(coarse_rows)
            for i, slot in enumerate(range(at, at + count))
        ]
        f = terms[9].astype(jnp.bfloat16)
        for slot, level in ((8, 4), (7, 3), (6, 2)):
            f = (terms[slot] + mm(cmaps[rows[level]], f)).astype(jnp.bfloat16)
        for i in range(2):
            g = (terms[4 + i] + mm(cmaps[rows[1] + i], f)).astype(jnp.bfloat16)
            for j in range(2):
                n = 2 * i + j
                whole = terms[n] + mm(cmaps[rows[0] + n], g)
                f1_out[phase, n] = pack(whole, 0)
        for o in range(1, 8):
            f1_copy(phase, o).start()
        f1_in[phase, z] = f1_out[phase, z]

    def f1_copy(phase, o):
        tz = lax.rem(z + o // 2, 4)
        to = (line * 4 + tz) * 2 + lax.rem(c + o % 2, 2)
        return remote(
            f1_out.at[phase, tz],
            f1_in.at[phase, z],
            f1_send.at[phase],
            f1_recv.at[phase],
            to,
        )

    def exchange(phase):
        if phase == 0:
            lax.fori_loop(0, LEAVES, turn_basis, 0, unroll=4)
            lax.fori_loop(0, LEAVES * LEAF // COLS, mark, 0, unroll=4)

        if phase == 0:
            loads[9].wait()

            @pl.when(is_server)
            def _():
                serve(phase)


        def pair(t, carry):
            near_leaf(phase, 2 * t, False)
            near_leaf(phase, 2 * t + 1, False)
            return carry

        lax.fori_loop(1, LEAVES // 2 - 1, pair, 0)
        for h in halo_copies(phase):
            h.wait_recv()

        def edge_pair(i, carry):
            near_leaf(phase, i * (LEAVES - HALO), True)
            near_leaf(phase, i * (LEAVES - HALO) + 1, True)
            return carry

        lax.fori_loop(0, 2, edge_pair, 0)
        if phase == 1:

            @pl.when(is_server)
            def _():
                serve(phase)

    def finish(phase):
        take(recv[phase].at[pl.ds(0, DEV - 1)], block_recv.at[phase])

        def couple(t, bits):
            kids = jnp.concatenate(
                [
                    recv[phase][within(lax.shift_right_logical(sources_s[k, t], bits), DEV)]
                    for k in range(4)
                ],
                axis=0,
            )
            coupled[t] = mm(blocks[t], kids)

        def leaf_pair(t, carry):
            couple(t, 4)
            return carry

        for t in range(NODES - 1, LEAVES - 1, -1):
            height = max(h for h in range(5) if t >= STARTS[h])
            couple(t, 4 - height)
        lax.fori_loop(0, LEAVES, leaf_pair, 0, unroll=4)

        @pl.when(jnp.logical_not(is_server))
        def _():
            take(f1_in.at[phase], f1_recv.at[phase])

        @pl.when(is_server)
        def _():
            take(f1_in.at[phase, pl.ds(0, 3)], f1_recv.at[phase])

        field[NODES - 1] = (
            coupled[NODES - 1] + mm(maps[NODES - 1], join(f1_in, phase))
        ).astype(jnp.bfloat16)
        for height in range(3, -1, -1):
            for j in range(LEAVES >> (height + 1)):
                lo = STARTS[height] + 2 * j
                pushed = mm(
                    maps[lo : lo + 2].reshape(2 * RANK, RANK),
                    field[STARTS[height + 1] + j],
                )
                both = coupled[lo : lo + 2] + pushed.reshape(2, RANK, COLS)
                field[lo : lo + 2] = both.astype(jnp.bfloat16)

    def first_leaf(t, carry):
        rows = pl.ds(pl.multiple_of(t * LEAF, LEAF), LEAF)
        score = acc[rows, :] + mm(basis_t[t], field[t])
        marked = shift[rows, :].astype(jnp.float32)
        middle = w[rows, :] + (marked - 0.25 * jnp.tanh(0.5 * score))
        based[rows, :] = middle + marked
        v = middle.astype(jnp.bfloat16)
        vals1[t] = v
        return carry

    def second_coef(t, carry):
        coef[t] = mm(basis[t], vals1[t]).astype(jnp.bfloat16)
        return carry

    map_copy.start()
    mate_copy(0).start()

    far_first(me, list_copy)

    @pl.when(is_server)
    def _():
        prepare_server()

    take(requests.at[pl.ds(0, DEV - 1)], list_sem.at[1])
    mine = (lax.broadcasted_iota(jnp.int32, (8, DEV), 1) == me).astype(jnp.bfloat16)
    asks = requests[...].reshape(DEV, COLS).astype(jnp.float32).astype(jnp.bfloat16)
    wanted = lax.dot_general(
        mine, asks, (((1,), (1,)), ((), ())), preferred_element_type=jnp.float32
    )
    chosen_v[...] = jnp.clip(wanted, 0, NODES - 1).astype(jnp.int32)
    small = pltpu.make_async_copy(chosen_v, chosen, small_sem)
    small.start()
    send_top(0)
    small.wait()
    fill(0, 2)
    send_blocks(0, 0, 2)
    fill(2, BATCHES)
    recv0[me] = coef[within(chosen[0, me], NODES)]
    send_blocks(0, 2, 8)
    for h in halo_copies(0):
        h.start()
    send_blocks(0, 8, BATCHES)
    exchange(0)
    finish(0)
    lax.fori_loop(0, LEAVES, first_leaf, 0, unroll=4)
    for h in halo_copies(1):
        h.start()
    lax.fori_loop(0, LEAVES, second_coef, 0, unroll=4)

    blocks_sent(0)
    mate_copy(0).wait_send()
    climb()
    mate_copy(1).start()
    fill(0, 2)
    send_blocks(1, 0, 2)
    fill(2, BATCHES)
    recv1[me] = coef[within(chosen[0, me], NODES)]
    send_top(1)
    send_blocks(1, 2, BATCHES)
    exchange(1)
    finish(1)

    map_copy.wait_send()
    take(requests.at[pl.ds(0, DEV - 1)], list_sem.at[0])
    mate_copy(1).wait_send()
    blocks_sent(1)
    for phase in range(2):
        for h in halo_copies(phase):
            h.wait_send()
        take(packed[phase].at[pl.ds(0, 32)], gather_send.at[phase])

        @pl.when(is_server)
        def _():
            take(packed[phase].at[pl.ds(0, 7)], f1_send.at[phase])


def last_kernel(based, near_term, field, basis_t, updated_h, scores_h, updated, scores, sem):
    copies = []
    for part in range(4):
        for t in range(4 * part, 4 * part + 4):
            rows = pl.ds(t * LEAF, LEAF)
            score = near_term[rows, :] + mm(basis_t[t], field[t])
            scores[rows, :] = score
            updated[rows, :] = based[rows, :] - 0.25 * jnp.tanh(0.5 * score)
        rows = pl.ds(4 * part * LEAF, 4 * LEAF)
        for i, (src, dst) in enumerate(((updated, updated_h), (scores, scores_h))):
            copies.append(
                pltpu.make_async_copy(src.at[rows], dst.at[rows], sem.at[i, part])
            )
            copies[-1].start()
    for copy in copies:
        copy.wait()


def local(
    weights,
    labels,
    basis,
    near_tiles,
    near_ids,
    transfer,
    couplings,
    sources,
    coarse_transfer,
    coarse_couplings,
    coarse_sources,
):
    bf16, f32, i32 = jnp.bfloat16, jnp.float32, jnp.int32
    points = LEAVES * LEAF
    vmem = pl.BlockSpec(memory_space=pltpu.VMEM)
    hbm = pl.BlockSpec(memory_space=pl.ANY)
    dma = pltpu.SemaphoreType.DMA
    scratch = [
        pltpu.SMEM((4, NODES), i32),
        pltpu.SMEM((2, LEAVES), i32),
        pltpu.SMEM((4, COARSE), i32),
        pltpu.VMEM((4, NODES), i32),
        pltpu.VMEM((points // COLS, COLS), i32),
        pltpu.VMEM((points, COLS), f32),
        pltpu.VMEM((points, COLS), bf16),
        pltpu.VMEM((LEAVES, LEAF, COLS), bf16),
        pltpu.VMEM((LEAVES, LEAF, COLS), bf16),
        pltpu.VMEM((2 * HALO, LEAF, COLS), bf16),
        pltpu.VMEM((2 * HALO, LEAF, COLS), bf16),
        pltpu.VMEM((LEAVES, 3, LEAF, LEAF), bf16),
        pltpu.VMEM((LEAVES, RANK, LEAF), bf16),
        pltpu.VMEM((NODES, RANK, RANK), bf16),
        pltpu.VMEM((16, RANK, 2 * RANK), bf16),
        pltpu.VMEM((NODES, RANK, 4 * RANK), bf16),
        pltpu.VMEM((NODES, RANK, COLS), bf16),
        pltpu.VMEM((NODES, RANK, COLS), f32),
        pltpu.VMEM((DEV, RANK, COLS), bf16),
        pltpu.VMEM((DEV, RANK, COLS), bf16),
        pltpu.VMEM((DEV, RANK, COLS), bf16),
        pltpu.VMEM((1, COLS), i32),
        pltpu.VMEM((DEV, 1, COLS), i32),
        pltpu.VMEM((8, DEV), i32),
        pltpu.SMEM((8, DEV), i32),
        pltpu.VMEM((RANK, RANK), bf16),
        pltpu.VMEM((2, RANK, COLS), bf16),
        pltpu.VMEM((2, 4, 16, COLS), bf16),
        pltpu.VMEM((64, 16, COLS), bf16),
        pltpu.VMEM((64, 16, COLS), bf16),
        pltpu.VMEM((COARSE, RANK, COLS), bf16),
        pltpu.VMEM((RANK, RANK, COARSE - 2), bf16),
        pltpu.VMEM(((RANK + 1) * (COARSE - 2), RANK), f32),
        pltpu.VMEM((COARSE - 2, RANK, RANK), bf16),
        pltpu.VMEM((62, RANK, 2 * RANK), bf16),
        pltpu.VMEM((10, RANK, 4 * RANK), bf16),
        pltpu.VMEM((2, 4, 16, COLS), bf16),
        pltpu.VMEM((2, 4, 16, COLS), bf16),
        dma((10,)),
        dma((7,)),
        dma((2,)),
        dma((2, 2)),
        dma((2, 2)),
        dma((3, 2)),
        dma((2,)),
        dma((2,)),
        dma((2,)),
        dma((2,)),
        dma((2,)),
        dma((2,)),
        dma(()),
    ]
    parts = pl.pallas_call(
        kernel,
        out_shape=(
            pltpu.VMEM((points, COLS), f32),
            pltpu.VMEM((points, COLS), f32),
            pltpu.VMEM((NODES, RANK, COLS), bf16),
            pltpu.VMEM((LEAVES, LEAF, RANK), bf16),
        ),
        in_specs=[hbm] * 11,
        out_specs=(vmem, vmem, vmem, vmem),
        scratch_shapes=scratch,
        compiler_params=pltpu.CompilerParams(
            collective_id=0, has_side_effects=True, vmem_limit_bytes=58 << 20
        ),
    )(
        sources.T,
        near_ids.T,
        coarse_sources.T,
        labels.reshape(points // COLS, COLS),
        weights,
        basis,
        near_tiles,
        transfer,
        couplings,
        coarse_transfer.transpose(1, 2, 0),
        coarse_couplings,
    )
    return pl.pallas_call(
        last_kernel,
        out_shape=(
            jax.ShapeDtypeStruct((points, COLS), f32),
            jax.ShapeDtypeStruct((points, COLS), f32),
        ),
        in_specs=[vmem] * 4,
        out_specs=(hbm, hbm),
        scratch_shapes=[
            pltpu.VMEM((points, COLS), f32),
            pltpu.VMEM((points, COLS), f32),
            dma((2, 4)),
        ],
        compiler_params=pltpu.CompilerParams(vmem_limit_bytes=16 << 20),
    )(*parts)


def solution(mesh):
    in_specs = (
        P("leaf", None),
        P("leaf"),
        P("leaf", None, None),
        P("leaf", None, None, None),
        P("leaf", None),
        P("leaf", None, None),
        P("leaf", None, None),
        P("leaf", None),
        P(),
        P(),
        P(),
    )
    out_specs = (P("leaf", None), P("leaf", None))
    return jax.shard_map(local, mesh=mesh, in_specs=in_specs, out_specs=out_specs, check_vma=False)
```
